32 devices in a mesh: section: 2 (over x), req: 8 (over z, y), head: 2 (over core).
Axes of the slice: x: 2, y: 2, z: 4, core: 2. Of those that a mesh axis runs over, the one named last changes fastest.
Arguments:
- latent_tokens: bfloat16 [8, 2, 256, 1536], P('req', None, 'head'), may hold values from -6 to 6
- w_qkv: bfloat16 [2, 1536, 4608], P('section', 'req', 'head'), may hold values from -0.15625 to 0.15625
- w_out: bfloat16 [2, 1536, 1536], P('section', 'head', 'req'), may hold values from -0.75 to 0.75
- time_mod: float32 [2, 28, 3, 1536], P('section'), may hold values from -3 to 3
- text_mod: float32 [2, 8, 2, 3, 1536], P('section', 'req'), may hold values from -3 to 3
- stale_kv: bfloat16 [2, 8, 2, 1178, 3072], P('section', 'req', None, None, 'head'), may hold values from -150 to 150
- guided: int32 [8], P('req'), may hold values 0 or 1
- patch_index: int32 [8], P('req'), may hold values from 0 to 3
- timestep: int32 [8], P('req'), may hold values from 0 to 27
Outputs:
- hidden_out: bfloat16 [2, 8, 2, 256, 1536], P('section', 'req', None, 'head')
- fresh_kv: bfloat16 [2, 8, 2, 256, 3072], P('section', 'req', None, None, 'head')
The draws below stay inside these ranges and needn't reach their ends.
All inputs are finite; a program needn't handle non-finite values. No bound on the sum of `guided` on one device may be relied on, other than what follows from the above.
Results may differ from the reference program's by a relative error of at most 0.04.
Values may be sent and summed in bfloat16 or wider, within the bound.
A program may use at most 192 MiB of HBM per device.

```python
import jax
import jax.numpy as jnp
from jax import lax

D = 1536
HEADS = 24
HD = 64
PATCH = 256
PATCHES = 4
TSTEPS = 28
LAYERS = 2
REQS = 8
STALE = 1178
N_HEAD = 2


def draw_stale_kv(key, part):
    shape = (LAYERS, REQS, 2, STALE, 2 * D)
    base = jnp.clip(jax.random.normal(key, shape, jnp.float32), -6.0, 6.0)
    return base.astype(jnp.bfloat16)


def with_ends(entries, stream_key, low, top_value):
    place = [jax.random.randint(jax.random.fold_in(stream_key, axis), (), 0, length) for axis, length in enumerate(entries.shape)]
    main_axis = entries.shape.index(max(entries.shape))
    next_to = place[:main_axis] + [(place[main_axis] + 1) % entries.shape[main_axis]] + place[main_axis + 1:]
    return entries.at[tuple(place)].set(low).at[tuple(next_to)].set(top_value)


def block_scale(rng, shape, pieces, smallest, high):
    factor_of, own = 1.0, jax.random.fold_in(rng, 6)
    for dim, blocks in pieces:
        steps = jnp.exp(jax.random.uniform(jax.random.fold_in(own, dim), (blocks,), jnp.float32, smallest / len(pieces), high / len(pieces)))
        factor_of = factor_of * jnp.repeat(steps, shape[dim] // blocks).reshape([-1 if axis == dim else 1 for axis in range(len(shape))])
    return factor_of


def scatter_about(key, dims, deviation, bound, shards=(), kind=jnp.bfloat16):
    gain = block_scale(key, dims, shards, -0.22, 0.18) if shards else 1.0
    array = jax.random.normal(key, dims, jnp.float32) * deviation * gain
    return jnp.minimum(jnp.maximum(array, -bound), bound).astype(kind)


def setup_inputs(seed: int = 0) -> dict:
    seeds = jax.random.split(jax.random.key(seed), 10)
    latent_tokens = scatter_about(seeds[0], (REQS, 2, PATCH, D), 1.0, 6.0, ((0, 8), (2, 2)))
    w_qkv = scatter_about(seeds[1], (LAYERS, D, 3 * D), D ** -0.5, 0.15625, ((0, 2), (1, 8), (2, 2)))
    w_out = scatter_about(seeds[2], (LAYERS, D, D), HD ** -0.5, 0.75, ((0, 2), (1, 2), (2, 8)))
    time_mod = scatter_about(seeds[3], (LAYERS, TSTEPS, 3, D), 0.5, 3.0, ((0, 2),), jnp.float32)
    text_mod = scatter_about(seeds[4], (LAYERS, REQS, 2, 3, D), 0.5, 3.0, ((0, 2), (1, 8)), jnp.float32)
    stale_kv = draw_stale_kv(jax.random.fold_in(seeds[9], 71), 0)
    guided = with_ends((jax.random.randint(seeds[6], (REQS,), 0, 2) < 1).astype(jnp.int32), jax.random.fold_in(seeds[6], 1), 0, 1)
    patch_index = with_ends(jax.random.randint(seeds[7], (REQS,), 0, PATCHES), jax.random.fold_in(seeds[7], 1), 0, PATCHES - 1).astype(jnp.int32)
    timestep = with_ends(jax.random.randint(seeds[8], (REQS,), 0, TSTEPS), jax.random.fold_in(seeds[8], 1), 0, TSTEPS - 1).astype(jnp.int32)
    return {"latent_tokens": latent_tokens, "w_qkv": w_qkv, "w_out": w_out, "time_mod": time_mod, "text_mod": text_mod, "stale_kv": stale_kv, "guided": guided, "patch_index": patch_index, "timestep": timestep}


def attend(queries, own_keys, own_values, stale_pair, patch_here):
    heads_here = queries.shape[1]
    stale_split = stale_pair.reshape(STALE, heads_here, 2, HD)
    stale_keys = stale_split[:, :, 0]
    stale_values = stale_split[:, :, 1]
    all_keys = jnp.concatenate([own_keys, stale_keys], 0)
    all_values = jnp.concatenate([own_values, stale_values], 0)
    scores = jnp.einsum('qhd,khd->hqk', queries.astype(jnp.float32), all_keys.astype(jnp.float32)) * HD ** (-0.5)
    position = jnp.arange(PATCH + STALE, dtype=jnp.int32)
    stale_pos = position - PATCH
    hidden_key = (stale_pos >= 0) & (stale_pos < PATCHES * PATCH) & (stale_pos // PATCH == patch_here)
    scores = jnp.where(hidden_key[None, None, :], -jnp.inf, scores)
    row_max = lax.optimization_barrier(jnp.max(scores, axis=-1, keepdims=True))
    exponent = jnp.exp(scores - row_max)
    weights = (exponent / lax.optimization_barrier(jnp.sum(exponent, axis=-1, keepdims=True))).astype(jnp.bfloat16)
    mixed_heads = jnp.einsum('hqk,khd->qhd', weights.astype(jnp.float32), all_values.astype(jnp.float32))
    return mixed_heads.astype(jnp.bfloat16).reshape(PATCH, heads_here * HD)

def apply_layer(hidden, qkv_weight, out_weight, modulation, stale_pair, patch_here):
    values_f = hidden.astype(jnp.float32)
    row_mean = lax.optimization_barrier(jnp.mean(values_f, axis=-1, keepdims=True))
    centered = values_f - row_mean
    row_var = lax.optimization_barrier(jnp.mean(centered * centered, axis=-1, keepdims=True))
    normed = (centered * lax.rsqrt(row_var + 1e-06) * (1.0 + modulation[1]) + modulation[0]).astype(jnp.bfloat16)
    projected = jnp.dot(normed, qkv_weight, preferred_element_type=jnp.float32).reshape(PATCH, HEADS, 3, HD)
    queries = projected[:, :, 0].astype(jnp.bfloat16)
    own_keys = projected[:, :, 1].astype(jnp.bfloat16)
    own_values = projected[:, :, 2].astype(jnp.bfloat16)
    mixed_heads = attend(queries, own_keys, own_values, stale_pair, patch_here)
    group_cols = D // N_HEAD
    partials = jnp.einsum('pgf,gfd->gpd', mixed_heads.reshape(PATCH, N_HEAD, group_cols).astype(jnp.float32), out_weight.reshape(N_HEAD, group_cols, D).astype(jnp.float32)).astype(jnp.bfloat16)
    attn_sum = lax.optimization_barrier(jnp.sum(partials.astype(jnp.float32), axis=0))
    updated = (values_f + modulation[2] * attn_sum).astype(jnp.bfloat16)
    fresh_pair = jnp.stack([own_keys, own_values], axis=2).reshape(PATCH, 2 * D)
    return (updated, fresh_pair)

def reference(latent_tokens, w_qkv, w_out, time_mod, text_mod, stale_kv, guided, patch_index, timestep):
    item_count = REQS * 2
    tokens = latent_tokens.reshape(item_count, PATCH, D)
    item_ids = jnp.arange(item_count, dtype=jnp.int32)
    request_of = item_ids // 2
    parity = item_ids % 2
    keep_row = jnp.where((parity == 1) & (guided[request_of] == 0), 0.0, 1.0).astype(jnp.float32)
    modulation = (time_mod[:, timestep][:, :, None] + text_mod).reshape(LAYERS, item_count, 3, D)
    stale_all = stale_kv.reshape(LAYERS, item_count, STALE, 2 * D)
    patch_all = patch_index[request_of]

    def one_item(item_index):
        hidden = tokens[item_index]
        layer_hidden = []
        layer_fresh = []
        for layer_index in range(LAYERS):
            hidden, fresh_pair = apply_layer(hidden, w_qkv[layer_index], w_out[layer_index], modulation[layer_index, item_index], stale_all[layer_index, item_index], patch_all[item_index])
            layer_hidden.append(hidden)
            layer_fresh.append(fresh_pair)
        factor = keep_row[item_index]
        kept_hidden = (jnp.stack(layer_hidden).astype(jnp.float32) * factor).astype(jnp.bfloat16)
        kept_fresh = (jnp.stack(layer_fresh).astype(jnp.float32) * factor).astype(jnp.bfloat16)
        return (kept_hidden, kept_fresh)
    all_hidden, all_fresh = lax.map(one_item, item_ids)
    hidden_out = jnp.transpose(all_hidden, (1, 0, 2, 3)).reshape(LAYERS, REQS, 2, PATCH, D)
    fresh_kv = jnp.transpose(all_fresh, (1, 0, 2, 3)).reshape(LAYERS, REQS, 2, PATCH, 2 * D)
    return (hidden_out, fresh_kv)
```

```python
import functools

import jax
import jax.numpy as jnp
from jax import lax
from jax.experimental import pallas as pl
from jax.experimental.pallas import tpu as pltpu
from jax.sharding import PartitionSpec as P

HD = 64
PATCH = 256
PATCHES = 4
STALE = 1178
TEXT = STALE - PATCHES * PATCH
MESH = pl.DeviceIdType.MESH


def ring_index(place, n):
    return jnp.where(place < n // 2, 2 * place, 2 * (n - 1 - place) + 1)


def nt_dot(a, b):
    return lax.dot_general(a, b, (((1,), (1,)), ((), ())), preferred_element_type=jnp.float32)


def cut(rows):
    unit = 16
    units = rows // unit
    first = (units + 1) // 2
    ways = []
    for begin, count in ((0, first), (first, units - first)):
        head = (count + 1) // 2
        spans = [(begin * unit, head * unit)]
        if count > head:
            spans.append(((begin + head) * unit, (count - head) * unit))
        ways.append(spans)
    return ways


def fused_kernel(
    n,
    heads,
    timestep,
    patch,
    guided,
    tokens,
    wq_in,
    wo_in,
    time_mod,
    text_mod,
    stale,
    hidden_out,
    fresh_out,
    wq,
    wo,
    raw,
    kv,
    ve,
    hbuf,
    normed,
    mixed,
    scores,
    tops,
    pscr,
    terms,
    inbox,
    mine,
    q_send,
    q_recv,
    o_send,
    o_recv,
    own_sem,
    t_send,
    t_recv,
    e_send,
    e_recv,
    x_send,
    x_recv,
    f_send,
    f_recv,
):
    me = lax.axis_index("req")
    head = lax.axis_index("head")
    section = lax.axis_index("section")
    place = jnp.where(me % 2 == 0, me // 2, n - 1 - me // 2)
    right = ring_index((place + 1) % n, n)
    left = ring_index((place + n - 1) % n, n)
    width = hbuf.shape[-1]
    rows = PATCH // heads
    heads_here = kv.shape[-1] // (2 * HD)
    group = 2 if heads_here % 2 == 0 else heads_here
    groups = heads_here // group
    chunk = 384 if width % 384 == 0 else width
    chunks = width // chunk

    own = [
        pltpu.make_async_copy(wq_in, wq.at[me], own_sem.at[0]),
        pltpu.make_async_copy(wo_in, wo.at[me], own_sem.at[1]),
        pltpu.make_async_copy(stale, raw, own_sem.at[2]),
    ]
    own_rows = pl.ds(pl.multiple_of(head * rows, rows), rows)
    own_tokens = [
        pltpu.make_async_copy(tokens.at[r], hbuf.at[r, own_rows], own_sem.at[3 + r])
        for r in range(2)
    ]

    barrier = pltpu.get_barrier_semaphore()
    for neighbour in (left, right):
        pl.semaphore_signal(barrier, inc=1, device_id={"req": neighbour}, device_id_type=MESH)
    for far in range(1, heads):
        peer = {"head": (head + far) % heads}
        pl.semaphore_signal(barrier, inc=1, device_id=peer, device_id_type=MESH)
    pl.semaphore_signal(barrier, inc=1, device_id={"section": 1 - section}, device_id_type=MESH)
    for copy in own:
        copy.start()

    @pl.when(section == 0)
    def _():
        for copy in own_tokens:
            copy.start()

    pl.semaphore_wait(barrier, 2 + heads)

    def hop(source, target, spans, send, recv, step, way, number, first=False):
        begin, count = spans[way][number]
        owner = ring_index((place + jnp.where(way == 0, n - step, step)) % n, n)
        span = pl.ds(begin, count)
        return pltpu.make_async_remote_copy(
            src_ref=source.at[span] if first else target.at[owner, span],
            dst_ref=target.at[owner, span],
            send_sem=send.at[way, number],
            recv_sem=recv.at[step, way, number],
            device_id={"req": right if way == 0 else left},
            device_id_type=MESH,
        )

    q_spans = cut(wq_in.shape[0])
    o_spans = cut(wo_in.shape[0])
    q_hop = functools.partial(hop, wq_in, wq, q_spans, q_send, q_recv)
    o_hop = functools.partial(hop, wo_in, wo, o_spans, o_send, o_recv)

    def pieces(spans):
        most = max(len(spans[0]), len(spans[1]))
        return [(way, k) for k in range(most) for way in range(2) if k < len(spans[way])]

    q_pieces, o_pieces = pieces(q_spans), pieces(o_spans)
    for way, k in q_pieces:
        q_hop(0, way, k, first=True).start()

    def token_copy(r, far, owner):
        span = pl.ds(pl.multiple_of(owner * rows, rows), rows)
        return pltpu.make_async_remote_copy(
            src_ref=tokens.at[r],
            dst_ref=hbuf.at[r, span],
            send_sem=t_send.at[r, far - 1],
            recv_sem=t_recv.at[r, far - 1],
            device_id={"head": (head + far) % heads},
            device_id_type=MESH,
        )

    @pl.when(section == 0)
    def _():
        for r in range(2):
            for far in range(1, heads):
                token_copy(r, far, head).start()

    def relay(make, kinds, step):
        for way, k in kinds:
            before = make(step - 1, way, k)
            before.wait_recv()
            before.wait_send()
            make(step, way, k).start()

    def settle(make, kinds):
        for way, k in kinds:
            last = make(n - 2, way, k)
            last.wait_recv()
            last.wait_send()

    patch_here = patch[0]
    lane2 = lax.broadcasted_iota(jnp.int32, (2, 1, 2 * HD), 2)
    text_pad = TEXT // 16 * 16

    def spread(block):
        @pl.when(block == 0)
        def _():
            own[2].wait()
            zero = jnp.zeros((2, PATCH - text_pad, kv.shape[-1]), kv.dtype)
            kv[:, (PATCHES - 1) * PATCH + text_pad :, :] = zero
            ve[:, (PATCHES - 1) * PATCH + text_pad :, :] = zero

        def lanes_of(c):
            return pl.ds(pl.multiple_of(c * 2 * HD, 2 * HD), 2 * HD)

        @pl.when(block < PATCHES - 1)
        def _():
            begin = (block + (block >= patch_here).astype(jnp.int32)) * PATCH
            into = pl.ds(pl.multiple_of(block * PATCH, PATCH), PATCH)

            def body(c, _):
                pair = jnp.swapaxes(raw[pl.ds(begin, PATCH), :, lanes_of(c)], 0, 1)
                kv[:, into, lanes_of(c)] = pair
                ve[:, into, lanes_of(c)] = jnp.where(lane2 < HD, jnp.bfloat16(1), pair)
                return 0

            lax.fori_loop(0, heads_here, body, 0)

        @pl.when(block == PATCHES - 1)
        def _():
            first = (PATCHES - 1) * PATCH

            def body(c, _):
                pair = jnp.swapaxes(raw[PATCHES * PATCH :, :, lanes_of(c)], 0, 1)
                kv[:, first : first + TEXT, lanes_of(c)] = pair
                ve[:, first : first + TEXT, lanes_of(c)] = jnp.where(
                    lane2 < HD, jnp.bfloat16(1), pair
                )
                return 0

            lax.fori_loop(0, heads_here, body, 0)

    def q_step(step, _):
        relay(q_hop, q_pieces, step)
        spread(step - 1)
        return 0

    lax.fori_loop(1, n - 1, q_step, 0)
    own[1].wait()
    for way, k in o_pieces:
        o_hop(0, way, k, first=True).start()
    settle(q_hop, q_pieces)
    own[0].wait()

    time_here = timestep[0]

    def modulation(k, r):
        return time_mod[time_here, k] + text_mod[k, pl.ds(r, 1), :]

    def onward(r, c, target):
        lanes = pl.ds(c * chunk, chunk)
        return pltpu.make_async_remote_copy(
            src_ref=mine.at[r, :, lanes],
            dst_ref=hbuf.at[r, own_rows, lanes],
            send_sem=x_send.at[r, c],
            recv_sem=x_recv.at[r, c],
            device_id={"section": target},
            device_id_type=MESH,
        )

    def forward(r, c, far, owner):
        span = pl.ds(pl.multiple_of(owner * rows, rows), rows)
        lanes = pl.ds(c * chunk, chunk)
        return pltpu.make_async_remote_copy(
            src_ref=hbuf.at[r, span, lanes],
            dst_ref=hbuf.at[r, span, lanes],
            send_sem=f_send.at[r, c, far - 1],
            recv_sem=f_recv.at[r, c, far - 1],
            device_id={"head": (head + far) % heads},
            device_id_type=MESH,
        )

    def take_tokens(r):
        @pl.when(section == 0)
        def _():
            pltpu.make_async_copy(tokens.at[r], hbuf.at[r, own_rows], own_sem.at[3 + r]).wait()
            for far in range(1, heads):
                token_copy(r, far, (head + heads - far) % heads).wait_recv()

        @pl.when(section == 1)
        def _():
            for c in range(chunks):
                onward(r, c, 0).wait_recv()
                for far in range(1, heads):
                    forward(r, c, far, head).start()
            for c in range(chunks):
                for far in range(1, heads):
                    forward(r, c, far, (head + heads - far) % heads).wait_recv()

    @pl.when(section == 1)
    def _():
        lax.fori_loop(1, n - 1, lambda s, _: (relay(o_hop, o_pieces, s), 0)[1], 0)
        settle(o_hop, o_pieces)

    keep = [jnp.float32(1.0), (guided[0] != 0).astype(jnp.float32)]
    lane = lax.broadcasted_iota(jnp.int32, (PATCH, PATCH), 1)
    lane1 = lax.broadcasted_iota(jnp.int32, (PATCH, 2 * HD), 1)
    blank = jnp.zeros((PATCH, HD), jnp.bfloat16)
    span = group * 3 * HD
    columns = wq.shape[0] * wq.shape[1]

    def row_body(r, _):
        take_tokens(r)
        values_f = hbuf[r].astype(jnp.float32)
        row_mean = jnp.mean(values_f, axis=-1, keepdims=True)
        centered = values_f - row_mean
        row_var = jnp.mean(centered * centered, axis=-1, keepdims=True)
        scaled = centered * lax.rsqrt(row_var + 1e-06)
        normed[...] = (scaled * (1.0 + modulation(1, r)) + modulation(0, r)).astype(jnp.bfloat16)
        keep_here = jnp.where(r == 0, keep[0], keep[1])

        def project(j):
            cols = pl.ds(pl.multiple_of(j * span, 128), span) if groups > 1 else slice(None)
            weight = wq[:, :, cols].reshape(columns, span)
            return jnp.dot(normed[...], weight, preferred_element_type=jnp.float32).astype(
                jnp.bfloat16
            )

        def lanes_of(j, h):
            return pl.ds(pl.multiple_of((j * group + h) * 2 * HD, 2 * HD), 2 * HD)

        def score(j, h, projected, slot):
            query = projected[:, h * 3 * HD : h * 3 * HD + HD]
            pair = projected[:, h * 3 * HD + HD : (h + 1) * 3 * HD]
            query = jnp.concatenate([query * jnp.bfloat16(HD**-0.5), blank], axis=1)
            most = None
            for b in range(PATCHES + 1):
                part = pair if b == 0 else kv[r, (b - 1) * PATCH : b * PATCH, lanes_of(j, h)]
                block = nt_dot(query, part)
                if b == PATCHES:
                    block = jnp.where(lane < TEXT, block, -jnp.inf)
                scores[slot, :, b * PATCH : (b + 1) * PATCH] = block
                here = jnp.maximum(block[:, :128], block[:, 128:])
                most = here if most is None else jnp.maximum(most, here)
            tops[slot] = jnp.broadcast_to(jnp.max(most, axis=-1, keepdims=True), (PATCH, 128))

        def mix(j, h, projected, slot):
            pair = projected[:, h * 3 * HD + HD : (h + 1) * 3 * HD]
            fresh_out[r, :, lanes_of(j, h)] = (pair.astype(jnp.float32) * keep_here).astype(
                jnp.bfloat16
            )
            top = tops[slot]
            top = jnp.concatenate([top, top], axis=1)
            total = None
            for b in range(PATCHES + 1):
                if b == 0:
                    value = jnp.where(lane1 < HD, jnp.bfloat16(1), pair)
                else:
                    value = ve[r, (b - 1) * PATCH : b * PATCH, lanes_of(j, h)]
                weight = jnp.exp(scores[slot, :, b * PATCH : (b + 1) * PATCH] - top)
                term = jnp.dot(
                    weight.astype(jnp.bfloat16), value, preferred_element_type=jnp.float32
                )
                total = term if total is None else total + term
            return (total[:, HD:] / total[:, :HD]).astype(jnp.bfloat16)

        first = project(0)
        pscr[...] = first
        score(0, 0, first, 0)

        def group_body(j, _):
            @pl.when(section == 0)
            def _():
                done = r * groups + j
                lo = 1 + done * (n - 2) // (2 * groups)
                hi = 1 + (done + 1) * (n - 2) // (2 * groups)
                lax.fori_loop(lo, hi, lambda s, _: (relay(o_hop, o_pieces, s), 0)[1], 0)

            projected = pscr[...]
            outs = []
            if groups > 1:
                following = jnp.minimum(j + 1, groups - 1)
                later = project(following)
            for h in range(group):
                if h + 1 < group:
                    score(j, h + 1, projected, (h + 1) % 2)
                elif groups > 1:
                    score(following, 0, later, 0)
                outs.append(mix(j, h, projected, h % 2))
            if groups > 1:
                pscr[...] = later
                cols = pl.ds(pl.multiple_of(j * group * HD, 128), group * HD)
            else:
                cols = slice(None)
            mixed[r, :, cols] = jnp.concatenate(outs, axis=1)
            return 0

        lax.fori_loop(0, groups, group_body, 0)
        return 0

    lax.fori_loop(0, 2, row_body, 0)

    @pl.when(section == 0)
    def _():
        settle(o_hop, o_pieces)

    def share(r, c, far):
        peer = (head + far) % heads
        lanes = pl.ds(c * chunk, chunk)
        return pltpu.make_async_remote_copy(
            src_ref=terms.at[r, pl.ds(pl.multiple_of(peer * rows, rows), rows), lanes],
            dst_ref=inbox.at[far - 1, r, :, lanes],
            send_sem=e_send.at[r, c, far - 1],
            recv_sem=e_recv.at[r, c, far - 1],
            device_id={"head": peer},
            device_id_type=MESH,
        )

    def finish(r, c):
        lanes = slice(c * chunk, (c + 1) * chunk)
        attn = terms[r, own_rows, lanes].astype(jnp.float32)
        for far in range(1, heads):
            share(r, c, far).wait_recv()
            attn = attn + inbox[far - 1, r, :, lanes].astype(jnp.float32)
        before = hbuf[r, own_rows, lanes].astype(jnp.float32)
        gate = modulation(2, r)[:, lanes]
        updated = (before + gate * attn).astype(jnp.bfloat16)
        hidden_out[r, :, lanes] = (updated.astype(jnp.float32) * keep[r]).astype(jnp.bfloat16)
        mine[r, :, lanes] = updated

        @pl.when(section == 0)
        def _():
            onward(r, c, 1).start()

    out_rows = wo.shape[0] * wo.shape[1]
    per = out_rows // chunks
    blocks = per // wo.shape[1] if per % wo.shape[1] == 0 else None
    order = [(r, c) for r in range(2) for c in range(chunks)]
    for number, (r, c) in enumerate(order):
        weight = wo[c * blocks : (c + 1) * blocks].reshape(per, wo.shape[2])
        terms[r, :, c * chunk : (c + 1) * chunk] = nt_dot(mixed[r], weight).astype(jnp.bfloat16)
        for far in range(1, heads):
            share(r, c, far).start()
        if number > 0:
            finish(*order[number - 1])
    finish(*order[-1])

    for r, c in order:
        for far in range(1, heads):
            share(r, c, far).wait_send()

    @pl.when(section == 0)
    def _():
        for r in range(2):
            for far in range(1, heads):
                token_copy(r, far, head).wait_send()
        for r, c in order:
            onward(r, c, 1).wait_send()

    @pl.when(section == 1)
    def _():
        for r, c in order:
            for far in range(1, heads):
                forward(r, c, far, head).wait_send()


def shards(
    latent_tokens, w_qkv, w_out, time_mod, text_mod, stale_kv, guided, patch_index, timestep
):
    n = lax.axis_size("req")
    heads = lax.axis_size("head")
    rows, width = latent_tokens.shape[2:]
    columns = stale_kv.shape[-1]
    bf16, f32 = jnp.bfloat16, jnp.float32
    chunks = width // (384 if width % 384 == 0 else width)
    heads_here = columns // (2 * HD)
    group = 2 if heads_here % 2 == 0 else heads_here
    dma = pltpu.SemaphoreType.DMA
    smem = pl.BlockSpec(memory_space=pltpu.SMEM)
    vmem = pl.BlockSpec(memory_space=pltpu.VMEM)
    hbm = pl.BlockSpec(memory_space=pl.ANY)
    keys = PATCHES * PATCH
    hidden, fresh = pl.pallas_call(
        functools.partial(fused_kernel, n, heads),
        out_shape=(
            jax.ShapeDtypeStruct((2, rows, width), bf16),
            jax.ShapeDtypeStruct((2, PATCH, columns), bf16),
        ),
        in_specs=[smem, smem, smem, hbm, hbm, hbm, vmem, vmem, hbm],
        out_specs=[vmem, vmem],
        scratch_shapes=[
            pltpu.VMEM((n, *w_qkv.shape[1:]), bf16),
            pltpu.VMEM((n, w_out.shape[2], w_out.shape[1]), bf16),
            pltpu.VMEM((STALE, 2, columns), bf16),
            pltpu.VMEM((2, keys, columns), bf16),
            pltpu.VMEM((2, keys, columns), bf16),
            pltpu.VMEM((2, PATCH, width), bf16),
            pltpu.VMEM((PATCH, width), bf16),
            pltpu.VMEM((2, PATCH, columns // 2), bf16),
            pltpu.VMEM((2, PATCH, keys + PATCH), f32),
            pltpu.VMEM((2, PATCH, 128), f32),
            pltpu.VMEM((PATCH, group * 3 * HD), bf16),
            pltpu.VMEM((2, PATCH, width), bf16),
            pltpu.VMEM((heads - 1, 2, rows, width), bf16),
            pltpu.VMEM((2, rows, width), bf16),
            dma((2, 2)),
            dma((n - 1, 2, 2)),
            dma((2, 2)),
            dma((n - 1, 2, 2)),
            dma((5,)),
            dma((2, heads - 1)),
            dma((2, heads - 1)),
            dma((2, chunks, heads - 1)),
            dma((2, chunks, heads - 1)),
            dma((2, chunks)),
            dma((2, chunks)),
            dma((2, chunks, heads - 1)),
            dma((2, chunks, heads - 1)),
        ],
        compiler_params=pltpu.CompilerParams(
            collective_id=0, has_side_effects=True, vmem_limit_bytes=58 << 20
        ),
    )(
        timestep,
        patch_index,
        guided,
        latent_tokens[0],
        w_qkv[0],
        w_out[0].T,
        jnp.transpose(time_mod, (1, 2, 0, 3)),
        jnp.swapaxes(text_mod[0, 0], 0, 1),
        jnp.swapaxes(stale_kv[0, 0], 0, 1),
    )
    return (hidden[None, None], fresh[None, None])


def solution(mesh):
    in_specs = (
        P("req", None, "head", None),
        P("section", "req", "head"),
        P("section", "head", "req"),
        P("section", None, None, None),
        P("section", "req", None, None, None),
        P("section", "req", None, None, "head"),
        P("req"),
        P("req"),
        P("req"),
    )
    out_specs = (P("section", "req", None, "head", None), P("section", "req", None, None, "head"))
    return jax.shard_map(shards, mesh=mesh, in_specs=in_specs, out_specs=out_specs, check_vma=False)
```

```python
import functools

import jax
import jax.numpy as jnp
from jax import lax
from jax.experimental import pallas as pl
from jax.experimental.pallas import tpu as pltpu
from jax.sharding import PartitionSpec as P

HD = 64
PATCH = 256
PATCHES = 4
STALE = 1178
TEXT = STALE - PATCHES * PATCH
MESH = pl.DeviceIdType.MESH


def ring_index(place, n):
    return jnp.where(place < n // 2, 2 * place, 2 * (n - 1 - place) + 1)


def nt_dot(a, b):
    return lax.dot_general(a, b, (((1,), (1,)), ((), ())), preferred_element_type=jnp.float32)


def cut(begin, rows):
    unit = 16
    units = rows // unit
    first = (units + 1) // 2
    ways = []
    for start, count in ((0, first), (first, units - first)):
        head = (count + 1) // 2
        spans = []
        if head > 0:
            spans.append((begin + start * unit, head * unit))
        if count > head:
            spans.append((begin + (start + head) * unit, (count - head) * unit))
        ways.append(spans)
    return ways


def order_of(spans):
    most = max(len(way) for way in spans)
    return [(way, k) for k in range(most) for way in range(2) if k < len(spans[way])]


def lent_rows(rows):
    return rows // 2 // 16 * 16


def fused_kernel(
    n,
    heads,
    timestep,
    patch,
    guided,
    tokens,
    wq_in,
    wo_in,
    time_mod,
    text_mod,
    stale,
    hidden_out,
    fresh_out,
    wq,
    wo,
    wx,
    raw,
    kv,
    ve,
    hbuf,
    normed,
    cut_0,
    cut_1,
    projected_all,
    mixed,
    scores,
    tops,
    pscr,
    terms,
    inbox,
    mine,
    q_send,
    q_recv,
    o_send,
    o_recv,
    w_send,
    w_recv,
    l_send,
    l_recv,
    g_sem,
    own_sem,
    t_send,
    t_recv,
    e_send,
    e_recv,
    x_send,
    x_recv,
    f_send,
    f_recv,
):
    me = lax.axis_index("req")
    head = lax.axis_index("head")
    section = lax.axis_index("section")
    place = jnp.where(me % 2 == 0, me // 2, n - 1 - me // 2)
    right = ring_index((place + 1) % n, n)
    left = ring_index((place + n - 1) % n, n)
    width = hbuf.shape[-1]
    rows = PATCH // heads
    heads_here = kv.shape[-1] // (2 * HD)
    group = 2 if heads_here % 2 == 0 else heads_here
    groups = heads_here // group
    chunk = 384 if width % 384 == 0 else width
    chunks = width // chunk
    q_rows, o_rows = wq_in.shape[0], wo_in.shape[0]
    lent = lent_rows(o_rows)
    kept_rows = o_rows - lent
    span = group * 3 * HD
    qkv_columns = wq_in.shape[1]

    own = [
        pltpu.make_async_copy(wq_in, wq.at[me], own_sem.at[0]),
        pltpu.make_async_copy(wo_in, wo.at[me], own_sem.at[1]),
        pltpu.make_async_copy(stale, raw, own_sem.at[2]),
    ]
    own_rows = pl.ds(pl.multiple_of(head * rows, rows), rows)
    own_tokens = [
        pltpu.make_async_copy(tokens.at[r], hbuf.at[r, own_rows], own_sem.at[3 + r])
        for r in range(2)
    ]

    barrier = pltpu.get_barrier_semaphore()
    for neighbour in (left, right):
        pl.semaphore_signal(barrier, inc=1, device_id={"req": neighbour}, device_id_type=MESH)
    for far in range(1, heads):
        peer = {"head": (head + far) % heads}
        pl.semaphore_signal(barrier, inc=1, device_id=peer, device_id_type=MESH)
    pl.semaphore_signal(barrier, inc=1, device_id={"section": 1 - section}, device_id_type=MESH)

    @pl.when(section == 0)
    def _():
        for copy in own_tokens:
            copy.start()

    for copy in own:
        copy.start()
    pl.semaphore_wait(barrier, 2 + heads)

    def hop(source, target, spans, shift, send, recv, step, way, number, first=False):
        begin, count = spans[way][number]
        owner = ring_index((place + (n - step if way == 0 else step)) % n, n)
        into = pl.ds(begin, count)
        return pltpu.make_async_remote_copy(
            src_ref=source.at[into] if first else target.at[owner, into],
            dst_ref=target.at[owner, into],
            send_sem=send.at[way, number],
            recv_sem=recv.at[step, way, number],
            device_id={"req": right if way == 0 else left},
            device_id_type=MESH,
        )

    def ring(source, target, spans, send, recv):
        return functools.partial(hop, source, target, spans, 0, send, recv), order_of(spans)

    q_spans = cut(0, q_rows)
    x_spans = cut(0, lent)
    q_ring = ring(wq_in, wq, q_spans, q_send, q_recv)
    part_ring = ring(wo_in, wo, cut(0, kept_rows), o_send, o_recv)
    whole_ring = ring(wo_in, wo, cut(0, o_rows), o_send, o_recv)
    x_ring = ring(wx.at[me], wx, x_spans, w_send, w_recv)

    def begin_ring(made):
        for way, k in made[1]:
            made[0](0, way, k, first=True).start()

    def relay(made, step):
        for way, k in made[1]:
            before = made[0](step - 1, way, k)
            before.wait_recv()
            before.wait_send()
            made[0](step, way, k).start()

    def relays(made, low, high):
        lax.fori_loop(low, high, lambda s, _: (relay(made, s), 0)[1], 0)

    def settle(made):
        for way, k in made[1]:
            last = made[0](n - 2, way, k)
            last.wait_recv()
            last.wait_send()

    def lend(target):
        return pltpu.make_async_remote_copy(
            src_ref=wo_in.at[pl.ds(kept_rows, lent)],
            dst_ref=wx.at[me],
            send_sem=g_sem.at[0],
            recv_sem=g_sem.at[1],
            device_id={"section": target},
            device_id_type=MESH,
        )

    def give_back(step, way, number, target):
        begin, count = x_spans[way][number]
        owner = ring_index((place + (n - 1 - step if way == 0 else step + 1)) % n, n)
        return pltpu.make_async_remote_copy(
            src_ref=wx.at[owner, pl.ds(begin, count)],
            dst_ref=wo.at[owner, pl.ds(kept_rows + begin, count)],
            send_sem=l_send.at[step, way, number],
            recv_sem=l_recv.at[step, way, number],
            device_id={"section": target},
            device_id_type=MESH,
        )

    def token_copy(r, far, owner):
        into = pl.ds(pl.multiple_of(owner * rows, rows), rows)
        return pltpu.make_async_remote_copy(
            src_ref=tokens.at[r],
            dst_ref=hbuf.at[r, into],
            send_sem=t_send.at[r, far - 1],
            recv_sem=t_recv.at[r, far - 1],
            device_id={"head": (head + far) % heads},
            device_id_type=MESH,
        )

    begin_ring(q_ring)

    patch_here = patch[0]
    lane2 = lax.broadcasted_iota(jnp.int32, (2, 1, 2 * HD), 2)
    text_pad = TEXT // 16 * 16

    def spread(block):
        @pl.when(block == 0)
        def _():
            own[2].wait()
            zero = jnp.zeros((2, PATCH - text_pad, kv.shape[-1]), kv.dtype)
            kv[:, (PATCHES - 1) * PATCH + text_pad :, :] = zero
            ve[:, (PATCHES - 1) * PATCH + text_pad :, :] = zero

        def lanes_of(c):
            return pl.ds(pl.multiple_of(c * 2 * HD, 2 * HD), 2 * HD)

        @pl.when(block < PATCHES - 1)
        def _():
            begin = (block + (block >= patch_here).astype(jnp.int32)) * PATCH
            into = pl.ds(pl.multiple_of(block * PATCH, PATCH), PATCH)

            def body(c, _):
                pair = jnp.swapaxes(raw[pl.ds(begin, PATCH), :, lanes_of(c)], 0, 1)
                kv[:, into, lanes_of(c)] = pair
                ve[:, into, lanes_of(c)] = jnp.where(lane2 < HD, jnp.bfloat16(1), pair)
                return 0

            lax.fori_loop(0, heads_here, body, 0)

        @pl.when(block == PATCHES - 1)
        def _():
            first = (PATCHES - 1) * PATCH

            def body(c, _):
                pair = jnp.swapaxes(raw[PATCHES * PATCH :, :, lanes_of(c)], 0, 1)
                kv[:, first : first + TEXT, lanes_of(c)] = pair
                ve[:, first : first + TEXT, lanes_of(c)] = jnp.where(
                    lane2 < HD, jnp.bfloat16(1), pair
                )
                return 0

            lax.fori_loop(0, heads_here, body, 0)

    time_here = timestep[0]

    def modulation(k, r):
        return time_mod[time_here, k] + text_mod[k, pl.ds(r, 1), :]

    def normalised(r):
        values_f = hbuf[r].astype(jnp.float32)
        row_mean = jnp.mean(values_f, axis=-1, keepdims=True)
        centered = values_f - row_mean
        row_var = jnp.mean(centered * centered, axis=-1, keepdims=True)
        scaled = centered * lax.rsqrt(row_var + 1e-06)
        return (scaled * (1.0 + modulation(1, r)) + modulation(0, r)).astype(jnp.bfloat16)

    def onward(r, c, target):
        lanes = pl.ds(c * chunk, chunk)
        return pltpu.make_async_remote_copy(
            src_ref=mine.at[r, :, lanes],
            dst_ref=hbuf.at[r, own_rows, lanes],
            send_sem=x_send.at[r, c],
            recv_sem=x_recv.at[r, c],
            device_id={"section": target},
            device_id_type=MESH,
        )

    def forward(r, c, far, owner):
        into = pl.ds(pl.multiple_of(owner * rows, rows), rows)
        lanes = pl.ds(c * chunk, chunk)
        return pltpu.make_async_remote_copy(
            src_ref=hbuf.at[r, into, lanes],
            dst_ref=hbuf.at[r, into, lanes],
            send_sem=f_send.at[r, c, far - 1],
            recv_sem=f_recv.at[r, c, far - 1],
            device_id={"head": (head + far) % heads},
            device_id_type=MESH,
        )

    keep = [jnp.float32(1.0), (guided[0] != 0).astype(jnp.float32)]
    lane = lax.broadcasted_iota(jnp.int32, (PATCH, PATCH), 1)
    lane1 = lax.broadcasted_iota(jnp.int32, (PATCH, 2 * HD), 1)
    blank = jnp.zeros((PATCH, HD), jnp.bfloat16)

    def columns_of(j):
        return pl.ds(pl.multiple_of(j * span, 128), span) if groups > 1 else slice(None)

    def lanes_of(j, h):
        return pl.ds(pl.multiple_of((j * group + h) * 2 * HD, 2 * HD), 2 * HD)

    def score(r, j, h, projected, slot):
        query = projected[:, h * 3 * HD : h * 3 * HD + HD]
        pair = projected[:, h * 3 * HD + HD : (h + 1) * 3 * HD]
        query = jnp.concatenate([query * jnp.bfloat16(HD**-0.5), blank], axis=1)
        most = None
        for b in range(PATCHES + 1):
            part = pair if b == 0 else kv[r, (b - 1) * PATCH : b * PATCH, lanes_of(j, h)]
            block = nt_dot(query, part)
            if b == PATCHES:
                block = jnp.where(lane < TEXT, block, -jnp.inf)
            scores[slot, :, b * PATCH : (b + 1) * PATCH] = block
            here = jnp.maximum(block[:, :128], block[:, 128:])
            most = here if most is None else jnp.maximum(most, here)
        tops[slot] = jnp.broadcast_to(jnp.max(most, axis=-1, keepdims=True), (PATCH, 128))

    def mix(r, j, h, projected, slot):
        keep_here = jnp.where(r == 0, keep[0], keep[1])
        pair = projected[:, h * 3 * HD + HD : (h + 1) * 3 * HD]
        fresh_out[r, :, lanes_of(j, h)] = (pair.astype(jnp.float32) * keep_here).astype(
            jnp.bfloat16
        )
        top = tops[slot]
        top = jnp.concatenate([top, top], axis=1)
        total = None
        for b in range(PATCHES + 1):
            if b == 0:
                value = jnp.where(lane1 < HD, jnp.bfloat16(1), pair)
            else:
                value = ve[r, (b - 1) * PATCH : b * PATCH, lanes_of(j, h)]
            weight = jnp.exp(scores[slot, :, b * PATCH : (b + 1) * PATCH] - top)
            term = jnp.dot(weight.astype(jnp.bfloat16), value, preferred_element_type=jnp.float32)
            total = term if total is None else total + term
        return (total[:, HD:] / total[:, :HD]).astype(jnp.bfloat16)

    def attend(r, project, beside):
        first = project(r, 0)
        pscr[...] = first
        score(r, 0, 0, first, 0)

        def group_body(j, _):
            beside(j)
            projected = pscr[...]
            outs = []
            if groups > 1:
                following = jnp.minimum(j + 1, groups - 1)
                later = project(r, following)
            for h in range(group):
                if h + 1 < group:
                    score(r, j, h + 1, projected, (h + 1) % 2)
                elif groups > 1:
                    score(r, following, 0, later, 0)
                outs.append(mix(r, j, h, projected, h % 2))
            if groups > 1:
                pscr[...] = later
                cols = pl.ds(pl.multiple_of(j * group * HD, 128), group * HD)
            else:
                cols = slice(None)
            mixed[r, :, cols] = jnp.concatenate(outs, axis=1)
            return 0

        lax.fori_loop(0, groups, group_body, 0)

    def share(r, c, far):
        peer = (head + far) % heads
        lanes = pl.ds(c * chunk, chunk)
        return pltpu.make_async_remote_copy(
            src_ref=terms.at[r, pl.ds(pl.multiple_of(peer * rows, rows), rows), lanes],
            dst_ref=inbox.at[far - 1, r, :, lanes],
            send_sem=e_send.at[r, c, far - 1],
            recv_sem=e_recv.at[r, c, far - 1],
            device_id={"head": peer},
            device_id_type=MESH,
        )

    def finish(r, c, sends):
        lanes = slice(c * chunk, (c + 1) * chunk)
        attn = terms[r, own_rows, lanes].astype(jnp.float32)
        for far in range(1, heads):
            share(r, c, far).wait_recv()
            attn = attn + inbox[far - 1, r, :, lanes].astype(jnp.float32)
        before = hbuf[r, own_rows, lanes].astype(jnp.float32)
        gate = modulation(2, r)[:, lanes]
        updated = (before + gate * attn).astype(jnp.bfloat16)
        hidden_out[r, :, lanes] = (updated.astype(jnp.float32) * keep[r]).astype(jnp.bfloat16)
        if sends:
            mine[r, :, lanes] = updated
            onward(r, c, 1).start()

    blocks = chunk // o_rows

    def put_out(some_rows, sends):
        order = [(r, c) for r in some_rows for c in range(chunks)]
        for number, (r, c) in enumerate(order):
            weight = wo[c * blocks : (c + 1) * blocks].reshape(chunk, wo.shape[2])
            terms[r, :, c * chunk : (c + 1) * chunk] = nt_dot(mixed[r], weight).astype(
                jnp.bfloat16
            )
            for far in range(1, heads):
                share(r, c, far).start()
            if number > 0:
                finish(*order[number - 1], sends)
        finish(*order[-1], sends)

    everything = [(r, c) for r in range(2) for c in range(chunks)]

    @pl.when(section == 0)
    def _():
        lend(1).start()
        for r in range(2):
            for far in range(1, heads):
                token_copy(r, far, head).start()
        cuts = (cut_0, cut_1)
        places = [
            (way[0][0], sum(count for _, count in way)) if way else None for way in q_spans
        ]
        for r in range(2):
            own_tokens[r].wait()
            for far in range(1, heads):
                token_copy(r, far, (head + heads - far) % heads).wait_recv()
            normed[...] = normalised(r)
            for way in range(2):
                if places[way] is not None:
                    begin, count = places[way]
                    for o in range(n):
                        cuts[way][o, r * PATCH : (r + 1) * PATCH, :] = normed[
                            :, o * q_rows + begin : o * q_rows + begin + count
                        ]

        tile = 768 if qkv_columns % 768 == 0 else qkv_columns

        def add_up(owner, way, start):
            if places[way] is None:
                return
            begin, count = places[way]

            def body(t, _):
                cols = (
                    pl.ds(pl.multiple_of(t * tile, 128), tile)
                    if tile < qkv_columns
                    else slice(None)
                )
                term = jnp.dot(
                    cuts[way][owner],
                    wq[owner, begin : begin + count, cols],
                    preferred_element_type=jnp.float32,
                )
                if start:
                    projected_all[:, cols] = term
                else:
                    projected_all[:, cols] += term
                return 0

            lax.fori_loop(0, qkv_columns // tile, body, 0)

        own[0].wait()
        for way in range(2):
            add_up(me, way, way == 0)

        def arrived(step):
            for way in range(2):
                owner = ring_index((place + (n - step if way == 0 else step)) % n, n)
                add_up(owner, way, False)

        def q_step(step, _):
            relay(q_ring, step)
            spread(step - 1)
            arrived(step)
            return 0

        lax.fori_loop(1, n - 1, q_step, 0)
        own[1].wait()
        begin_ring(part_ring)
        settle(q_ring)
        arrived(n - 1)

        def project(r, j):
            begin = pl.ds(pl.multiple_of(r * PATCH, PATCH), PATCH)
            return projected_all[begin, columns_of(j)].astype(jnp.bfloat16)

        def beside(j):
            relays(part_ring, 1 + j * (n - 2) // groups, 1 + (j + 1) * (n - 2) // groups)

        attend(0, project, beside)
        settle(part_ring)

        def back(step, _):
            for way, k in order_of(x_spans):
                give_back(step, way, k, 1).wait_recv()
            return 0

        lax.fori_loop(0, n - 1, back, 0)
        put_out([0], True)
        attend(1, project, lambda j: None)
        put_out([1], True)
        for r in range(2):
            for far in range(1, heads):
                token_copy(r, far, head).wait_send()
        for r, c in everything:
            onward(r, c, 1).wait_send()
        lend(1).wait_send()

    @pl.when(section == 1)
    def _():
        lend(0).wait_recv()
        begin_ring(x_ring)

        def hand_back(step):
            for way, k in order_of(x_spans):
                give_back(step, way, k, 0).start()

        def q_step(step, _):
            relay(q_ring, step)
            relay(x_ring, step)
            hand_back(step - 1)
            spread(step - 1)
            return 0

        lax.fori_loop(1, n - 1, q_step, 0)
        own[1].wait()
        begin_ring(whole_ring)
        settle(q_ring)
        settle(x_ring)
        hand_back(n - 2)
        own[0].wait()
        early = n // 2
        relays(whole_ring, 1, early)

        def project(r, j):
            weight = wq[:, :, columns_of(j)].reshape(n * q_rows, span)
            return jnp.dot(normed[...], weight, preferred_element_type=jnp.float32).astype(
                jnp.bfloat16
            )

        def row_body(r, _):
            for c in range(chunks):
                onward(r, c, 0).wait_recv()
                for far in range(1, heads):
                    forward(r, c, far, head).start()
            for c in range(chunks):
                for far in range(1, heads):
                    forward(r, c, far, (head + heads - far) % heads).wait_recv()
            normed[...] = normalised(r)

            def beside(j):
                done = jnp.minimum(r * groups + j, groups)
                later = jnp.minimum(r * groups + j + 1, groups)
                left_over = n - 1 - early
                relays(
                    whole_ring,
                    early + done * left_over // groups,
                    early + later * left_over // groups,
                )

            attend(r, project, beside)
            return 0

        lax.fori_loop(0, 2, row_body, 0)
        settle(whole_ring)
        put_out([0, 1], False)

        def handed(step, _):
            for way, k in order_of(x_spans):
                give_back(step, way, k, 0).wait_send()
            return 0

        lax.fori_loop(0, n - 1, handed, 0)
        for r, c in everything:
            for far in range(1, heads):
                forward(r, c, far, head).wait_send()

    for r, c in everything:
        for far in range(1, heads):
            share(r, c, far).wait_send()


def shards(
    latent_tokens, w_qkv, w_out, time_mod, text_mod, stale_kv, guided, patch_index, timestep
):
    n = lax.axis_size("req")
    heads = lax.axis_size("head")
    rows, width = latent_tokens.shape[2:]
    columns = stale_kv.shape[-1]
    bf16, f32 = jnp.bfloat16, jnp.float32
    chunks = width // (384 if width % 384 == 0 else width)
    heads_here = columns // (2 * HD)
    group = 2 if heads_here % 2 == 0 else heads_here
    dma = pltpu.SemaphoreType.DMA
    smem = pl.BlockSpec(memory_space=pltpu.SMEM)
    vmem = pl.BlockSpec(memory_space=pltpu.VMEM)
    hbm = pl.BlockSpec(memory_space=pl.ANY)
    keys = PATCHES * PATCH
    lent = lent_rows(w_out.shape[2])
    counts = [sum(count for _, count in way) for way in cut(0, w_qkv.shape[1])]
    hidden, fresh = pl.pallas_call(
        functools.partial(fused_kernel, n, heads),
        out_shape=(
            jax.ShapeDtypeStruct((2, rows, width), bf16),
            jax.ShapeDtypeStruct((2, PATCH, columns), bf16),
        ),
        in_specs=[smem, smem, smem, hbm, hbm, hbm, vmem, vmem, hbm],
        out_specs=[vmem, vmem],
        scratch_shapes=[
            pltpu.VMEM((n, *w_qkv.shape[1:]), bf16),
            pltpu.VMEM((n, w_out.shape[2], w_out.shape[1]), bf16),
            pltpu.VMEM((n, lent, w_out.shape[1]), bf16),
            pltpu.VMEM((STALE, 2, columns), bf16),
            pltpu.VMEM((2, keys, columns), bf16),
            pltpu.VMEM((2, keys, columns), bf16),
            pltpu.VMEM((2, PATCH, width), bf16),
            pltpu.VMEM((PATCH, width), bf16),
            *[pltpu.VMEM((n, 2 * PATCH, max(16, count)), bf16) for count in counts],
            pltpu.VMEM((2 * PATCH, w_qkv.shape[2]), f32),
            pltpu.VMEM((2, PATCH, columns // 2), bf16),
            pltpu.VMEM((2, PATCH, keys + PATCH), f32),
            pltpu.VMEM((2, PATCH, 128), f32),
            pltpu.VMEM((PATCH, group * 3 * HD), bf16),
            pltpu.VMEM((2, PATCH, width), bf16),
            pltpu.VMEM((heads - 1, 2, rows, width), bf16),
            pltpu.VMEM((2, rows, width), bf16),
            dma((2, 2)),
            dma((n - 1, 2, 2)),
            dma((2, 2)),
            dma((n - 1, 2, 2)),
            dma((2, 2)),
            dma((n - 1, 2, 2)),
            dma((n - 1, 2, 2)),
            dma((n - 1, 2, 2)),
            dma((2,)),
            dma((5,)),
            dma((2, heads - 1)),
            dma((2, heads - 1)),
            dma((2, chunks, heads - 1)),
            dma((2, chunks, heads - 1)),
            dma((2, chunks)),
            dma((2, chunks)),
            dma((2, chunks, heads - 1)),
            dma((2, chunks, heads - 1)),
        ],
        compiler_params=pltpu.CompilerParams(
            collective_id=0, has_side_effects=True, vmem_limit_bytes=58 << 20
        ),
    )(
        timestep,
        patch_index,
        guided,
        latent_tokens[0],
        w_qkv[0],
        w_out[0].T,
        jnp.transpose(time_mod, (1, 2, 0, 3)),
        jnp.swapaxes(text_mod[0, 0], 0, 1),
        jnp.swapaxes(stale_kv[0, 0], 0, 1),
    )
    return (hidden[None, None], fresh[None, None])


def solution(mesh):
    in_specs = (
        P("req", None, "head", None),
        P("section", "req", "head"),
        P("section", "head", "req"),
        P("section", None, None, None),
        P("section", "req", None, None, None),
        P("section", "req", None, None, "head"),
        P("req"),
        P("req"),
        P("req"),
    )
    out_specs = (P("section", "req", None, "head", None), P("section", "req", None, None, "head"))
    return jax.shard_map(shards, mesh=mesh, in_specs=in_specs, out_specs=out_specs, check_vma=False)
```

```python
import functools

import jax
import jax.numpy as jnp
from jax import lax
from jax.experimental import pallas as pl
from jax.experimental.pallas import tpu as pltpu
from jax.sharding import PartitionSpec as P

HD = 64
PATCH = 256
PATCHES = 4
STALE = 1178
TEXT = STALE - PATCHES * PATCH
MESH = pl.DeviceIdType.MESH


def ring_index(place, n):
    return jnp.where(place < n // 2, 2 * place, 2 * (n - 1 - place) + 1)


def nt_dot(a, b):
    return lax.dot_general(a, b, (((1,), (1,)), ((), ())), preferred_element_type=jnp.float32)


def cut(begin, rows):
    unit = 16
    units = rows // unit
    first = (units + 1) // 2
    ways = []
    for start, count in ((0, first), (first, units - first)):
        head = (count + 1) // 2
        spans = []
        if head > 0:
            spans.append((begin + start * unit, head * unit))
        if count > head:
            spans.append((begin + (start + head) * unit, (count - head) * unit))
        ways.append(spans)
    return ways


def order_of(spans):
    most = max(len(way) for way in spans)
    return [(way, k) for k in range(most) for way in range(2) if k < len(spans[way])]


def lent_rows(rows):
    return rows // 2 // 16 * 16


def fused_kernel(
    n,
    heads,
    timestep,
    patch,
    guided,
    tokens,
    wq_in,
    wo_in,
    time_in,
    text_mod,
    stale,
    hidden_to,
    fresh_to,
    hidden_out,
    fresh_out,
    time_mod,
    wq,
    wo,
    wx,
    raw,
    kv,
    ve,
    hbuf,
    normed,
    cut_0,
    cut_1,
    projected_all,
    mixed,
    scores,
    tops,
    pscr,
    terms,
    inbox,
    mine,
    q_send,
    q_recv,
    o_send,
    o_recv,
    w_send,
    w_recv,
    l_send,
    l_recv,
    g_sem,
    own_sem,
    t_send,
    t_recv,
    e_send,
    e_recv,
    x_send,
    x_recv,
    f_send,
    f_recv,
):
    me = lax.axis_index("req")
    head = lax.axis_index("head")
    section = lax.axis_index("section")
    place = jnp.where(me % 2 == 0, me // 2, n - 1 - me // 2)
    right = ring_index((place + 1) % n, n)
    left = ring_index((place + n - 1) % n, n)
    width = hbuf.shape[-1]
    rows = PATCH // heads
    heads_here = kv.shape[-1] // (2 * HD)
    group = 2 if heads_here % 2 == 0 else heads_here
    groups = heads_here // group
    chunk = 384 if width % 384 == 0 else width
    chunks = width // chunk
    q_rows, o_rows = wq_in.shape[0], wo_in.shape[0]
    lent = lent_rows(o_rows)
    kept_rows = o_rows - lent
    span = group * 3 * HD
    qkv_columns = wq_in.shape[1]

    own = [
        pltpu.make_async_copy(wq_in, wq.at[me], own_sem.at[0]),
        pltpu.make_async_copy(wo_in, wo.at[me], own_sem.at[1]),
        pltpu.make_async_copy(stale, raw, own_sem.at[2]),
    ]
    own_rows = pl.ds(pl.multiple_of(head * rows, rows), rows)
    time_copy = pltpu.make_async_copy(time_in, time_mod, own_sem.at[5])
    time_copy.start()

    def write_hidden(r):
        return pltpu.make_async_copy(hidden_out.at[r], hidden_to.at[r], own_sem.at[6 + r])

    def write_fresh(r):
        return pltpu.make_async_copy(fresh_out.at[r], fresh_to.at[r], own_sem.at[8 + r])

    own_tokens = [
        pltpu.make_async_copy(tokens.at[r], hbuf.at[r, own_rows], own_sem.at[3 + r])
        for r in range(2)
    ]

    barrier = pltpu.get_barrier_semaphore()
    for neighbour in (left, right):
        pl.semaphore_signal(barrier, inc=1, device_id={"req": neighbour}, device_id_type=MESH)
    for far in range(1, heads):
        peer = {"head": (head + far) % heads}
        pl.semaphore_signal(barrier, inc=1, device_id=peer, device_id_type=MESH)
    pl.semaphore_signal(barrier, inc=1, device_id={"section": 1 - section}, device_id_type=MESH)

    @pl.when(section == 0)
    def _():
        for copy in own_tokens:
            copy.start()

    for copy in own:
        copy.start()
    pl.semaphore_wait(barrier, 2 + heads)

    def hop(source, target, spans, shift, send, recv, step, way, number, first=False):
        begin, count = spans[way][number]
        owner = ring_index((place + (n - step if way == 0 else step)) % n, n)
        into = pl.ds(begin, count)
        return pltpu.make_async_remote_copy(
            src_ref=source.at[into] if first else target.at[owner, into],
            dst_ref=target.at[owner, into],
            send_sem=send.at[way, number],
            recv_sem=recv.at[step, way, number],
            device_id={"req": right if way == 0 else left},
            device_id_type=MESH,
        )

    def ring(source, target, spans, send, recv):
        return functools.partial(hop, source, target, spans, 0, send, recv), order_of(spans)

    q_spans = cut(0, q_rows)
    x_spans = cut(0, lent)
    q_ring = ring(wq_in, wq, q_spans, q_send, q_recv)
    part_ring = ring(wo_in, wo, cut(0, kept_rows), o_send, o_recv)
    whole_ring = ring(wo_in, wo, cut(0, o_rows), o_send, o_recv)
    x_ring = ring(wx.at[me], wx, x_spans, w_send, w_recv)

    def begin_ring(made):
        for way, k in made[1]:
            made[0](0, way, k, first=True).start()

    def relay(made, step):
        for way, k in made[1]:
            before = made[0](step - 1, way, k)
            before.wait_recv()
            before.wait_send()
            made[0](step, way, k).start()

    def relays(made, low, high):
        lax.fori_loop(low, high, lambda s, _: (relay(made, s), 0)[1], 0)

    def settle(made):
        for way, k in made[1]:
            last = made[0](n - 2, way, k)
            last.wait_recv()
            last.wait_send()

    def lend(target):
        return pltpu.make_async_remote_copy(
            src_ref=wo_in.at[pl.ds(kept_rows, lent)],
            dst_ref=wx.at[me],
            send_sem=g_sem.at[0],
            recv_sem=g_sem.at[1],
            device_id={"section": target},
            device_id_type=MESH,
        )

    def give_back(step, way, number, target):
        begin, count = x_spans[way][number]
        owner = ring_index((place + (n - 1 - step if way == 0 else step + 1)) % n, n)
        return pltpu.make_async_remote_copy(
            src_ref=wx.at[owner, pl.ds(begin, count)],
            dst_ref=wo.at[owner, pl.ds(kept_rows + begin, count)],
            send_sem=l_send.at[step, way, number],
            recv_sem=l_recv.at[step, way, number],
            device_id={"section": target},
            device_id_type=MESH,
        )

    def token_copy(r, far, owner):
        into = pl.ds(pl.multiple_of(owner * rows, rows), rows)
        return pltpu.make_async_remote_copy(
            src_ref=tokens.at[r],
            dst_ref=hbuf.at[r, into],
            send_sem=t_send.at[r, far - 1],
            recv_sem=t_recv.at[r, far - 1],
            device_id={"head": (head + far) % heads},
            device_id_type=MESH,
        )

    begin_ring(q_ring)

    patch_here = patch[0]
    lane2 = lax.broadcasted_iota(jnp.int32, (2, 1, 2 * HD), 2)
    text_pad = TEXT // 16 * 16

    def spread(block):
        @pl.when(block == 0)
        def _():
            own[2].wait()
            zero = jnp.zeros((2, PATCH - text_pad, kv.shape[-1]), kv.dtype)
            kv[:, (PATCHES - 1) * PATCH + text_pad :, :] = zero
            ve[:, (PATCHES - 1) * PATCH + text_pad :, :] = zero

        def lanes_of(c):
            return pl.ds(pl.multiple_of(c * 2 * HD, 2 * HD), 2 * HD)

        @pl.when(block < PATCHES - 1)
        def _():
            begin = (block + (block >= patch_here).astype(jnp.int32)) * PATCH
            into = pl.ds(pl.multiple_of(block * PATCH, PATCH), PATCH)

            def body(c, _):
                pair = jnp.swapaxes(raw[pl.ds(begin, PATCH), :, lanes_of(c)], 0, 1)
                kv[:, into, lanes_of(c)] = pair
                ve[:, into, lanes_of(c)] = jnp.where(lane2 < HD, jnp.bfloat16(1), pair)
                return 0

            lax.fori_loop(0, heads_here, body, 0)

        @pl.when(block == PATCHES - 1)
        def _():
            first = (PATCHES - 1) * PATCH

            def body(c, _):
                pair = jnp.swapaxes(raw[PATCHES * PATCH :, :, lanes_of(c)], 0, 1)
                kv[:, first : first + TEXT, lanes_of(c)] = pair
                ve[:, first : first + TEXT, lanes_of(c)] = jnp.where(
                    lane2 < HD, jnp.bfloat16(1), pair
                )
                return 0

            lax.fori_loop(0, heads_here, body, 0)

    time_here = timestep[0]

    def modulation(k, r):
        return time_mod[time_here, k] + text_mod[k, pl.ds(r, 1), :]

    def normalised(r):
        values_f = hbuf[r].astype(jnp.float32)
        row_mean = jnp.mean(values_f, axis=-1, keepdims=True)
        centered = values_f - row_mean
        row_var = jnp.mean(centered * centered, axis=-1, keepdims=True)
        scaled = centered * lax.rsqrt(row_var + 1e-06)
        return (scaled * (1.0 + modulation(1, r)) + modulation(0, r)).astype(jnp.bfloat16)

    def onward(r, c, target):
        lanes = pl.ds(c * chunk, chunk)
        return pltpu.make_async_remote_copy(
            src_ref=mine.at[r, :, lanes],
            dst_ref=hbuf.at[r, own_rows, lanes],
            send_sem=x_send.at[r, c],
            recv_sem=x_recv.at[r, c],
            device_id={"section": target},
            device_id_type=MESH,
        )

    def forward(r, c, far, owner):
        into = pl.ds(pl.multiple_of(owner * rows, rows), rows)
        lanes = pl.ds(c * chunk, chunk)
        return pltpu.make_async_remote_copy(
            src_ref=hbuf.at[r, into, lanes],
            dst_ref=hbuf.at[r, into, lanes],
            send_sem=f_send.at[r, c, far - 1],
            recv_sem=f_recv.at[r, c, far - 1],
            device_id={"head": (head + far) % heads},
            device_id_type=MESH,
        )

    keep = [jnp.float32(1.0), (guided[0] != 0).astype(jnp.float32)]
    lane = lax.broadcasted_iota(jnp.int32, (PATCH, PATCH), 1)
    lane1 = lax.broadcasted_iota(jnp.int32, (PATCH, 2 * HD), 1)
    blank = jnp.zeros((PATCH, HD), jnp.bfloat16)

    def columns_of(j):
        return pl.ds(pl.multiple_of(j * span, 128), span) if groups > 1 else slice(None)

    def lanes_of(j, h):
        return pl.ds(pl.multiple_of((j * group + h) * 2 * HD, 2 * HD), 2 * HD)

    def score(r, j, h, projected, slot):
        query = projected[:, h * 3 * HD : h * 3 * HD + HD]
        pair = projected[:, h * 3 * HD + HD : (h + 1) * 3 * HD]
        query = jnp.concatenate([query * jnp.bfloat16(HD**-0.5), blank], axis=1)
        most = None
        for b in range(PATCHES + 1):
            part = pair if b == 0 else kv[r, (b - 1) * PATCH : b * PATCH, lanes_of(j, h)]
            block = nt_dot(query, part)
            if b == PATCHES:
                block = jnp.where(lane < TEXT, block, -jnp.inf)
            scores[slot, :, b * PATCH : (b + 1) * PATCH] = block
            here = jnp.maximum(block[:, :128], block[:, 128:])
            most = here if most is None else jnp.maximum(most, here)
        tops[slot] = jnp.broadcast_to(jnp.max(most, axis=-1, keepdims=True), (PATCH, 128))

    def mix(r, j, h, projected, slot):
        keep_here = jnp.where(r == 0, keep[0], keep[1])
        pair = projected[:, h * 3 * HD + HD : (h + 1) * 3 * HD]
        fresh_out[r, :, lanes_of(j, h)] = (pair.astype(jnp.float32) * keep_here).astype(
            jnp.bfloat16
        )
        top = tops[slot]
        top = jnp.concatenate([top, top], axis=1)
        total = None
        for b in range(PATCHES + 1):
            if b == 0:
                value = jnp.where(lane1 < HD, jnp.bfloat16(1), pair)
            else:
                value = ve[r, (b - 1) * PATCH : b * PATCH, lanes_of(j, h)]
            weight = jnp.exp(scores[slot, :, b * PATCH : (b + 1) * PATCH] - top)
            term = jnp.dot(weight.astype(jnp.bfloat16), value, preferred_element_type=jnp.float32)
            total = term if total is None else total + term
        return (total[:, HD:] / total[:, :HD]).astype(jnp.bfloat16)

    def attend(r, project, beside):
        first = project(r, 0)
        pscr[...] = first
        score(r, 0, 0, first, 0)

        def group_body(j, _):
            beside(j)
            projected = pscr[...]
            outs = []
            if groups > 1:
                following = jnp.minimum(j + 1, groups - 1)
                later = project(r, following)
            for h in range(group):
                if h + 1 < group:
                    score(r, j, h + 1, projected, (h + 1) % 2)
                elif groups > 1:
                    score(r, following, 0, later, 0)
                outs.append(mix(r, j, h, projected, h % 2))
            if groups > 1:
                pscr[...] = later
                cols = pl.ds(pl.multiple_of(j * group * HD, 128), group * HD)
            else:
                cols = slice(None)
            mixed[r, :, cols] = jnp.concatenate(outs, axis=1)
            return 0

        lax.fori_loop(0, groups, group_body, 0)

    def share(r, c, far):
        peer = (head + far) % heads
        lanes = pl.ds(c * chunk, chunk)
        return pltpu.make_async_remote_copy(
            src_ref=terms.at[r, pl.ds(pl.multiple_of(peer * rows, rows), rows), lanes],
            dst_ref=inbox.at[far - 1, r, :, lanes],
            send_sem=e_send.at[r, c, far - 1],
            recv_sem=e_recv.at[r, c, far - 1],
            device_id={"head": peer},
            device_id_type=MESH,
        )

    def finish(r, c, sends):
        lanes = slice(c * chunk, (c + 1) * chunk)
        attn = terms[r, own_rows, lanes].astype(jnp.float32)
        for far in range(1, heads):
            share(r, c, far).wait_recv()
            attn = attn + inbox[far - 1, r, :, lanes].astype(jnp.float32)
        before = hbuf[r, own_rows, lanes].astype(jnp.float32)
        gate = modulation(2, r)[:, lanes]
        updated = (before + gate * attn).astype(jnp.bfloat16)
        hidden_out[r, :, lanes] = (updated.astype(jnp.float32) * keep[r]).astype(jnp.bfloat16)
        if sends:
            mine[r, :, lanes] = updated
            onward(r, c, 1).start()

    blocks = chunk // o_rows

    def put_out(some_rows, sends):
        order = [(r, c) for r in some_rows for c in range(chunks)]
        for number, (r, c) in enumerate(order):
            weight = wo[c * blocks : (c + 1) * blocks].reshape(chunk, wo.shape[2])
            terms[r, :, c * chunk : (c + 1) * chunk] = nt_dot(mixed[r], weight).astype(
                jnp.bfloat16
            )
            for far in range(1, heads):
                share(r, c, far).start()
            if number > 0:
                finish(*order[number - 1], sends)
        finish(*order[-1], sends)

    everything = [(r, c) for r in range(2) for c in range(chunks)]

    @pl.when(section == 0)
    def _():
        lend(1).start()
        for r in range(2):
            for far in range(1, heads):
                token_copy(r, far, head).start()
        time_copy.wait()
        cuts = (cut_0, cut_1)
        places = [
            (way[0][0], sum(count for _, count in way)) if way else None for way in q_spans
        ]
        for r in range(2):
            own_tokens[r].wait()
            for far in range(1, heads):
                token_copy(r, far, (head + heads - far) % heads).wait_recv()
            normed[...] = normalised(r)
            for way in range(2):
                if places[way] is not None:
                    begin, count = places[way]
                    for o in range(n):
                        cuts[way][o, r * PATCH : (r + 1) * PATCH, :] = normed[
                            :, o * q_rows + begin : o * q_rows + begin + count
                        ]

        tile = 768 if qkv_columns % 768 == 0 else qkv_columns

        def add_up(owner, way, start):
            if places[way] is None:
                return
            begin, count = places[way]

            def body(t, _):
                cols = (
                    pl.ds(pl.multiple_of(t * tile, 128), tile)
                    if tile < qkv_columns
                    else slice(None)
                )
                term = jnp.dot(
                    cuts[way][owner],
                    wq[owner, begin : begin + count, cols],
                    preferred_element_type=jnp.float32,
                )
                if start:
                    projected_all[:, cols] = term
                else:
                    projected_all[:, cols] += term
                return 0

            lax.fori_loop(0, qkv_columns // tile, body, 0)

        own[0].wait()
        for way in range(2):
            add_up(me, way, way == 0)

        def arrived(step):
            for way in range(2):
                owner = ring_index((place + (n - step if way == 0 else step)) % n, n)
                add_up(owner, way, False)

        lead = n // 4

        def q_step(step, _):
            relay(q_ring, step)

            @pl.when(step == lead)
            def _():
                begin_ring(part_ring)

            @pl.when(step > lead)
            def _():
                relay(part_ring, step - lead)

            spread(step - 1)
            arrived(step)
            return 0

        lax.fori_loop(1, n - 1, q_step, 0)
        own[1].wait()
        settle(q_ring)
        relay(part_ring, n - 1 - lead)
        arrived(n - 1)

        def project(r, j):
            begin = pl.ds(pl.multiple_of(r * PATCH, PATCH), PATCH)
            return projected_all[begin, columns_of(j)].astype(jnp.bfloat16)

        def beside(j):
            low = jnp.minimum(j * (lead - 1) // 2, lead - 1)
            high = jnp.minimum((j + 1) * (lead - 1) // 2, lead - 1)
            relays(part_ring, n - lead + low, n - lead + high)

        attend(0, project, beside)
        relays(part_ring, n - lead + jnp.minimum(groups * (lead - 1) // 2, lead - 1), n - 1)
        write_fresh(0).start()
        settle(part_ring)

        def back(step, _):
            for way, k in order_of(x_spans):
                give_back(step, way, k, 1).wait_recv()
            return 0

        lax.fori_loop(0, n - 1, back, 0)
        put_out([0], True)
        write_hidden(0).start()
        attend(1, project, lambda j: None)
        write_fresh(1).start()
        put_out([1], True)
        write_hidden(1).start()
        for r in range(2):
            for far in range(1, heads):
                token_copy(r, far, head).wait_send()
        for r, c in everything:
            onward(r, c, 1).wait_send()
        lend(1).wait_send()

    @pl.when(section == 1)
    def _():
        lend(0).wait_recv()
        begin_ring(x_ring)

        def hand_back(step):
            for way, k in order_of(x_spans):
                give_back(step, way, k, 0).start()

        def x_step(step):
            @pl.when(step < n - 1)
            def _():
                relay(x_ring, step)
                hand_back(step - 1)

            @pl.when(step == n - 1)
            def _():
                settle(x_ring)
                hand_back(n - 2)

        lead = n // 2
        q_first = [kind for kind in q_ring[1] if kind[1] == 0]
        q_rest = [kind for kind in q_ring[1] if kind[1] > 0]

        def q_step(step, _):
            x_step(2 * step - 1)
            relay((q_ring[0], q_first), step)
            x_step(2 * step)
            relay((q_ring[0], q_rest), step)

            @pl.when(step == lead)
            def _():
                begin_ring(whole_ring)

            @pl.when(step > lead)
            def _():
                relay(whole_ring, step - lead)

            spread(step - 1)
            return 0

        lax.fori_loop(1, n - 1, q_step, 0)
        own[1].wait()
        time_copy.wait()
        settle(q_ring)
        own[0].wait()
        early = n - lead
        relays(whole_ring, n - 1 - lead, early)

        def project(r, j):
            weight = wq[:, :, columns_of(j)].reshape(n * q_rows, span)
            return jnp.dot(normed[...], weight, preferred_element_type=jnp.float32).astype(
                jnp.bfloat16
            )

        def row_body(r, _):
            for c in range(chunks):
                onward(r, c, 0).wait_recv()
                for far in range(1, heads):
                    forward(r, c, far, head).start()
            for c in range(chunks):
                for far in range(1, heads):
                    forward(r, c, far, (head + heads - far) % heads).wait_recv()
            normed[...] = normalised(r)

            def beside(j):
                done = jnp.minimum(r * groups + j, groups)
                later = jnp.minimum(r * groups + j + 1, groups)
                left_over = n - 1 - early
                relays(
                    whole_ring,
                    early + done * left_over // groups,
                    early + later * left_over // groups,
                )

            attend(r, project, beside)
            write_fresh(r).start()
            return 0

        lax.fori_loop(0, 2, row_body, 0)
        settle(whole_ring)
        put_out([0, 1], False)
        for r in range(2):
            write_hidden(r).start()

        def handed(step, _):
            for way, k in order_of(x_spans):
                give_back(step, way, k, 0).wait_send()
            return 0

        lax.fori_loop(0, n - 1, handed, 0)
        for r, c in everything:
            for far in range(1, heads):
                forward(r, c, far, head).wait_send()

    for r, c in everything:
        for far in range(1, heads):
            share(r, c, far).wait_send()
    for r in range(2):
        write_fresh(r).wait()
        write_hidden(r).wait()


def shards(
    latent_tokens, w_qkv, w_out, time_mod, text_mod, stale_kv, guided, patch_index, timestep
):
    n = lax.axis_size("req")
    heads = lax.axis_size("head")
    rows, width = latent_tokens.shape[2:]
    columns = stale_kv.shape[-1]
    bf16, f32 = jnp.bfloat16, jnp.float32
    chunks = width // (384 if width % 384 == 0 else width)
    heads_here = columns // (2 * HD)
    group = 2 if heads_here % 2 == 0 else heads_here
    dma = pltpu.SemaphoreType.DMA
    smem = pl.BlockSpec(memory_space=pltpu.SMEM)
    vmem = pl.BlockSpec(memory_space=pltpu.VMEM)
    hbm = pl.BlockSpec(memory_space=pl.ANY)
    keys = PATCHES * PATCH
    lent = lent_rows(w_out.shape[2])
    counts = [sum(count for _, count in way) for way in cut(0, w_qkv.shape[1])]
    hidden, fresh = pl.pallas_call(
        functools.partial(fused_kernel, n, heads),
        out_shape=(
            jax.ShapeDtypeStruct((2, rows, width), bf16),
            jax.ShapeDtypeStruct((2, PATCH, columns), bf16),
        ),
        in_specs=[smem, smem, smem, hbm, hbm, hbm, hbm, vmem, hbm],
        out_specs=[hbm, hbm],
        scratch_shapes=[
            pltpu.VMEM((2, rows, width), bf16),
            pltpu.VMEM((2, PATCH, columns), bf16),
            pltpu.VMEM((time_mod.shape[1], time_mod.shape[2], 1, width), f32),
            pltpu.VMEM((n, *w_qkv.shape[1:]), bf16),
            pltpu.VMEM((n, w_out.shape[2], w_out.shape[1]), bf16),
            pltpu.VMEM((n, lent, w_out.shape[1]), bf16),
            pltpu.VMEM((STALE, 2, columns), bf16),
            pltpu.VMEM((2, keys, columns), bf16),
            pltpu.VMEM((2, keys, columns), bf16),
            pltpu.VMEM((2, PATCH, width), bf16),
            pltpu.VMEM((PATCH, width), bf16),
            *[pltpu.VMEM((n, 2 * PATCH, max(16, count)), bf16) for count in counts],
            pltpu.VMEM((2 * PATCH, w_qkv.shape[2]), f32),
            pltpu.VMEM((2, PATCH, columns // 2), bf16),
            pltpu.VMEM((2, PATCH, keys + PATCH), f32),
            pltpu.VMEM((2, PATCH, 128), f32),
            pltpu.VMEM((PATCH, group * 3 * HD), bf16),
            pltpu.VMEM((2, PATCH, width), bf16),
            pltpu.VMEM((heads - 1, 2, rows, width), bf16),
            pltpu.VMEM((2, rows, width), bf16),
            dma((2, 2)),
            dma((n - 1, 2, 2)),
            dma((2, 2)),
            dma((n - 1, 2, 2)),
            dma((2, 2)),
            dma((n - 1, 2, 2)),
            dma((n - 1, 2, 2)),
            dma((n - 1, 2, 2)),
            dma((2,)),
            dma((10,)),
            dma((2, heads - 1)),
            dma((2, heads - 1)),
            dma((2, chunks, heads - 1)),
            dma((2, chunks, heads - 1)),
            dma((2, chunks)),
            dma((2, chunks)),
            dma((2, chunks, heads - 1)),
            dma((2, chunks, heads - 1)),
        ],
        compiler_params=pltpu.CompilerParams(
            collective_id=0, has_side_effects=True, vmem_limit_bytes=58 << 20
        ),
    )(
        timestep,
        patch_index,
        guided,
        latent_tokens[0],
        w_qkv[0],
        w_out[0].T,
        jnp.transpose(time_mod, (1, 2, 0, 3)),
        jnp.swapaxes(text_mod[0, 0], 0, 1),
        jnp.swapaxes(stale_kv[0, 0], 0, 1),
    )
    return (hidden[None, None], fresh[None, None])


def solution(mesh):
    in_specs = (
        P("req", None, "head", None),
        P("section", "req", "head"),
        P("section", "head", "req"),
        P("section", None, None, None),
        P("section", "req", None, None, None),
        P("section", "req", None, None, "head"),
        P("req"),
        P("req"),
        P("req"),
    )
    out_specs = (P("section", "req", None, "head", None), P("section", "req", None, None, "head"))
    return jax.shard_map(shards, mesh=mesh, in_specs=in_specs, out_specs=out_specs, check_vma=False)
```

```python
import functools

import jax
import jax.numpy as jnp
from jax import lax
from jax.experimental import pallas as pl
from jax.experimental.pallas import tpu as pltpu
from jax.sharding import PartitionSpec as P

HD = 64
PATCH = 256
PATCHES = 4
STALE = 1178
TEXT = STALE - PATCHES * PATCH
MESH = pl.DeviceIdType.MESH


def ring_index(place, n):
    return jnp.where(place < n // 2, 2 * place, 2 * (n - 1 - place) + 1)


def nt_dot(a, b):
    return lax.dot_general(a, b, (((1,), (1,)), ((), ())), preferred_element_type=jnp.float32)


def cut(begin, rows):
    unit = 16
    units = rows // unit
    first = (units + 1) // 2
    ways = []
    for start, count in ((0, first), (first, units - first)):
        head = (count + 1) // 2
        spans = []
        if head > 0:
            spans.append((begin + start * unit, head * unit))
        if count > head:
            spans.append((begin + (start + head) * unit, (count - head) * unit))
        ways.append(spans)
    return ways


def order_of(spans):
    most = max(len(way) for way in spans)
    return [(way, k) for k in range(most) for way in range(2) if k < len(spans[way])]


def lent_rows(rows):
    return rows * 3 // 4 // 16 * 16


def fused_kernel(
    n,
    heads,
    timestep,
    patch,
    guided,
    tokens,
    wq_in,
    wo_in,
    time_in,
    text_mod,
    stale,
    hidden_to,
    fresh_to,
    hidden_out,
    fresh_out,
    time_mod,
    wq,
    wo,
    wx,
    raw,
    kv,
    ve,
    hbuf,
    normed,
    cut_0,
    cut_1,
    projected_all,
    mixed,
    scores,
    tops,
    pscr,
    terms,
    inbox,
    mine,
    q_send,
    q_recv,
    o_send,
    o_recv,
    w_send,
    w_recv,
    l_send,
    l_recv,
    g_sem,
    own_sem,
    t_send,
    t_recv,
    e_send,
    e_recv,
    x_send,
    x_recv,
    f_send,
    f_recv,
):
    me = lax.axis_index("req")
    head = lax.axis_index("head")
    section = lax.axis_index("section")
    place = jnp.where(me % 2 == 0, me // 2, n - 1 - me // 2)
    right = ring_index((place + 1) % n, n)
    left = ring_index((place + n - 1) % n, n)
    width = hbuf.shape[-1]
    rows = PATCH // heads
    heads_here = kv.shape[-1] // (2 * HD)
    group = 2 if heads_here % 2 == 0 else heads_here
    groups = heads_here // group
    chunk = 384 if width % 384 == 0 else width
    chunks = width // chunk
    q_rows, o_rows = wq_in.shape[0], wo_in.shape[0]
    lent = lent_rows(o_rows)
    kept_rows = o_rows - lent
    span = group * 3 * HD
    qkv_columns = wq_in.shape[1]

    own = [
        pltpu.make_async_copy(wq_in, wq.at[me], own_sem.at[0]),
        pltpu.make_async_copy(wo_in, wo.at[me], own_sem.at[1]),
        pltpu.make_async_copy(stale, raw, own_sem.at[2]),
    ]
    own_rows = pl.ds(pl.multiple_of(head * rows, rows), rows)
    time_copy = pltpu.make_async_copy(time_in, time_mod, own_sem.at[5])
    time_copy.start()

    def write_hidden(r):
        return pltpu.make_async_copy(hidden_out.at[r], hidden_to.at[r], own_sem.at[6 + r])

    def write_fresh(r):
        return pltpu.make_async_copy(fresh_out.at[r], fresh_to.at[r], own_sem.at[8 + r])

    own_tokens = [
        pltpu.make_async_copy(tokens.at[r], hbuf.at[r, own_rows], own_sem.at[3 + r])
        for r in range(2)
    ]

    barrier = pltpu.get_barrier_semaphore()
    for neighbour in (left, right):
        pl.semaphore_signal(barrier, inc=1, device_id={"req": neighbour}, device_id_type=MESH)
    for far in range(1, heads):
        peer = {"head": (head + far) % heads}
        pl.semaphore_signal(barrier, inc=1, device_id=peer, device_id_type=MESH)
    pl.semaphore_signal(barrier, inc=1, device_id={"section": 1 - section}, device_id_type=MESH)

    @pl.when(section == 0)
    def _():
        for copy in own_tokens:
            copy.start()

    for copy in own:
        copy.start()
    pl.semaphore_wait(barrier, 2 + heads)

    def hop(source, target, spans, shift, send, recv, step, way, number, first=False):
        begin, count = spans[way][number]
        owner = ring_index((place + (n - step if way == 0 else step)) % n, n)
        into = pl.ds(begin, count)
        return pltpu.make_async_remote_copy(
            src_ref=source.at[into] if first else target.at[owner, into],
            dst_ref=target.at[owner, into],
            send_sem=send.at[way, number],
            recv_sem=recv.at[step, way, number],
            device_id={"req": right if way == 0 else left},
            device_id_type=MESH,
        )

    def ring(source, target, spans, send, recv):
        return functools.partial(hop, source, target, spans, 0, send, recv), order_of(spans)

    q_spans = cut(0, q_rows)
    x_spans = cut(0, lent)
    q_ring = ring(wq_in, wq, q_spans, q_send, q_recv)
    part_ring = ring(wo_in, wo, cut(0, kept_rows), o_send, o_recv)
    whole_ring = ring(wo_in, wo, cut(0, o_rows), o_send, o_recv)
    x_ring = ring(wx.at[me], wx, x_spans, w_send, w_recv)

    def begin_ring(made):
        for way, k in made[1]:
            made[0](0, way, k, first=True).start()

    def relay(made, step):
        for way, k in made[1]:
            before = made[0](step - 1, way, k)
            before.wait_recv()
            before.wait_send()
            made[0](step, way, k).start()

    def relays(made, low, high):
        lax.fori_loop(low, high, lambda s, _: (relay(made, s), 0)[1], 0)

    def settle(made):
        for way, k in made[1]:
            last = made[0](n - 2, way, k)
            last.wait_recv()
            last.wait_send()

    def lend(target):
        return pltpu.make_async_remote_copy(
            src_ref=wo_in.at[pl.ds(kept_rows, lent)],
            dst_ref=wx.at[me],
            send_sem=g_sem.at[0],
            recv_sem=g_sem.at[1],
            device_id={"section": target},
            device_id_type=MESH,
        )

    def give_back(step, way, number, target):
        begin, count = x_spans[way][number]
        owner = ring_index((place + (n - 1 - step if way == 0 else step + 1)) % n, n)
        return pltpu.make_async_remote_copy(
            src_ref=wx.at[owner, pl.ds(begin, count)],
            dst_ref=wo.at[owner, pl.ds(kept_rows + begin, count)],
            send_sem=l_send.at[step, way, number],
            recv_sem=l_recv.at[step, way, number],
            device_id={"section": target},
            device_id_type=MESH,
        )

    def token_copy(r, far, owner):
        into = pl.ds(pl.multiple_of(owner * rows, rows), rows)
        return pltpu.make_async_remote_copy(
            src_ref=tokens.at[r],
            dst_ref=hbuf.at[r, into],
            send_sem=t_send.at[r, far - 1],
            recv_sem=t_recv.at[r, far - 1],
            device_id={"head": (head + far) % heads},
            device_id_type=MESH,
        )

    begin_ring(q_ring)

    patch_here = patch[0]
    lane2 = lax.broadcasted_iota(jnp.int32, (2, 1, 2 * HD), 2)
    text_pad = TEXT // 16 * 16

    def spread(block):
        @pl.when(block == 0)
        def _():
            own[2].wait()
            zero = jnp.zeros((2, PATCH - text_pad, kv.shape[-1]), kv.dtype)
            kv[:, (PATCHES - 1) * PATCH + text_pad :, :] = zero
            ve[:, (PATCHES - 1) * PATCH + text_pad :, :] = zero

        def lanes_of(c):
            return pl.ds(pl.multiple_of(c * 2 * HD, 2 * HD), 2 * HD)

        @pl.when(block < PATCHES - 1)
        def _():
            begin = (block + (block >= patch_here).astype(jnp.int32)) * PATCH
            into = pl.ds(pl.multiple_of(block * PATCH, PATCH), PATCH)

            def body(c, _):
                pair = jnp.swapaxes(raw[pl.ds(begin, PATCH), :, lanes_of(c)], 0, 1)
                kv[:, into, lanes_of(c)] = pair
                ve[:, into, lanes_of(c)] = jnp.where(lane2 < HD, jnp.bfloat16(1), pair)
                return 0

            lax.fori_loop(0, heads_here, body, 0)

        @pl.when(block == PATCHES - 1)
        def _():
            first = (PATCHES - 1) * PATCH

            def body(c, _):
                pair = jnp.swapaxes(raw[PATCHES * PATCH :, :, lanes_of(c)], 0, 1)
                kv[:, first : first + TEXT, lanes_of(c)] = pair
                ve[:, first : first + TEXT, lanes_of(c)] = jnp.where(
                    lane2 < HD, jnp.bfloat16(1), pair
                )
                return 0

            lax.fori_loop(0, heads_here, body, 0)

    time_here = timestep[0]

    def modulation(k, r):
        return time_mod[time_here, k] + text_mod[k, pl.ds(r, 1), :]

    def normalised(r):
        values_f = hbuf[r].astype(jnp.float32)
        row_mean = jnp.mean(values_f, axis=-1, keepdims=True)
        centered = values_f - row_mean
        row_var = jnp.mean(centered * centered, axis=-1, keepdims=True)
        scaled = centered * lax.rsqrt(row_var + 1e-06)
        return (scaled * (1.0 + modulation(1, r)) + modulation(0, r)).astype(jnp.bfloat16)

    def onward(r, c, target):
        lanes = pl.ds(c * chunk, chunk)
        return pltpu.make_async_remote_copy(
            src_ref=mine.at[r, :, lanes],
            dst_ref=hbuf.at[r, own_rows, lanes],
            send_sem=x_send.at[r, c],
            recv_sem=x_recv.at[r, c],
            device_id={"section": target},
            device_id_type=MESH,
        )

    def forward(r, c, far, owner):
        into = pl.ds(pl.multiple_of(owner * rows, rows), rows)
        lanes = pl.ds(c * chunk, chunk)
        return pltpu.make_async_remote_copy(
            src_ref=hbuf.at[r, into, lanes],
            dst_ref=hbuf.at[r, into, lanes],
            send_sem=f_send.at[r, c, far - 1],
            recv_sem=f_recv.at[r, c, far - 1],
            device_id={"head": (head + far) % heads},
            device_id_type=MESH,
        )

    keep = [jnp.float32(1.0), (guided[0] != 0).astype(jnp.float32)]
    lane = lax.broadcasted_iota(jnp.int32, (PATCH, PATCH), 1)
    lane1 = lax.broadcasted_iota(jnp.int32, (PATCH, 2 * HD), 1)
    blank = jnp.zeros((PATCH, HD), jnp.bfloat16)

    def columns_of(j):
        return pl.ds(pl.multiple_of(j * span, 128), span) if groups > 1 else slice(None)

    def lanes_of(j, h):
        return pl.ds(pl.multiple_of((j * group + h) * 2 * HD, 2 * HD), 2 * HD)

    def score(r, j, h, projected, slot):
        query = projected[:, h * 3 * HD : h * 3 * HD + HD]
        pair = projected[:, h * 3 * HD + HD : (h + 1) * 3 * HD]
        query = jnp.concatenate([query * jnp.bfloat16(HD**-0.5), blank], axis=1)
        most = None
        for b in range(PATCHES + 1):
            part = pair if b == 0 else kv[r, (b - 1) * PATCH : b * PATCH, lanes_of(j, h)]
            block = nt_dot(query, part)
            if b == PATCHES:
                block = jnp.where(lane < TEXT, block, -jnp.inf)
            scores[slot, :, b * PATCH : (b + 1) * PATCH] = block
            here = jnp.maximum(block[:, :128], block[:, 128:])
            most = here if most is None else jnp.maximum(most, here)
        tops[slot] = jnp.broadcast_to(jnp.max(most, axis=-1, keepdims=True), (PATCH, 128))

    def mix(r, j, h, projected, slot):
        keep_here = jnp.where(r == 0, keep[0], keep[1])
        pair = projected[:, h * 3 * HD + HD : (h + 1) * 3 * HD]
        fresh_out[r, :, lanes_of(j, h)] = (pair.astype(jnp.float32) * keep_here).astype(
            jnp.bfloat16
        )
        top = tops[slot]
        top = jnp.concatenate([top, top], axis=1)
        total = None
        for b in range(PATCHES + 1):
            if b == 0:
                value = jnp.where(lane1 < HD, jnp.bfloat16(1), pair)
            else:
                value = ve[r, (b - 1) * PATCH : b * PATCH, lanes_of(j, h)]
            weight = jnp.exp(scores[slot, :, b * PATCH : (b + 1) * PATCH] - top)
            term = jnp.dot(weight.astype(jnp.bfloat16), value, preferred_element_type=jnp.float32)
            total = term if total is None else total + term
        return (total[:, HD:] / total[:, :HD]).astype(jnp.bfloat16)

    def attend(r, project, beside):
        first = project(r, 0)
        pscr[...] = first
        score(r, 0, 0, first, 0)

        def group_body(j, _):
            beside(j)
            projected = pscr[...]
            outs = []
            if groups > 1:
                following = jnp.minimum(j + 1, groups - 1)
                later = project(r, following)
            for h in range(group):
                if h + 1 < group:
                    score(r, j, h + 1, projected, (h + 1) % 2)
                elif groups > 1:
                    score(r, following, 0, later, 0)
                outs.append(mix(r, j, h, projected, h % 2))
            if groups > 1:
                pscr[...] = later
                cols = pl.ds(pl.multiple_of(j * group * HD, 128), group * HD)
            else:
                cols = slice(None)
            mixed[r, :, cols] = jnp.concatenate(outs, axis=1)
            return 0

        lax.fori_loop(0, groups, group_body, 0)

    def share(r, c, far):
        peer = (head + far) % heads
        lanes = pl.ds(c * chunk, chunk)
        return pltpu.make_async_remote_copy(
            src_ref=terms.at[r, pl.ds(pl.multiple_of(peer * rows, rows), rows), lanes],
            dst_ref=inbox.at[far - 1, r, :, lanes],
            send_sem=e_send.at[r, c, far - 1],
            recv_sem=e_recv.at[r, c, far - 1],
            device_id={"head": peer},
            device_id_type=MESH,
        )

    def finish(r, c, sends):
        lanes = slice(c * chunk, (c + 1) * chunk)
        attn = terms[r, own_rows, lanes].astype(jnp.float32)
        for far in range(1, heads):
            share(r, c, far).wait_recv()
            attn = attn + inbox[far - 1, r, :, lanes].astype(jnp.float32)
        before = hbuf[r, own_rows, lanes].astype(jnp.float32)
        gate = modulation(2, r)[:, lanes]
        updated = (before + gate * attn).astype(jnp.bfloat16)
        hidden_out[r, :, lanes] = (updated.astype(jnp.float32) * keep[r]).astype(jnp.bfloat16)
        if sends:
            mine[r, :, lanes] = updated
            onward(r, c, 1).start()

    blocks = chunk // o_rows

    def put_out(some_rows, sends, lag):
        steps = [(r, c) for r in some_rows for c in range(chunks)]
        if len(some_rows) == 2:
            steps = [(None, c) for c in range(chunks)]
        waiting = []
        for r, c in steps:
            lanes = slice(c * chunk, (c + 1) * chunk)
            weight = wo[c * blocks : (c + 1) * blocks].reshape(chunk, wo.shape[2])
            if r is None:
                both = mixed[...].reshape(2 * PATCH, wo.shape[2])
                term = nt_dot(both, weight).astype(jnp.bfloat16)
                terms[:, :, lanes] = term.reshape(2, PATCH, chunk)
            else:
                terms[r, :, lanes] = nt_dot(mixed[r], weight).astype(jnp.bfloat16)
            for row in range(2) if r is None else [r]:
                for far in range(1, heads):
                    share(row, c, far).start()
                waiting.append((row, c))
            while len(waiting) > lag:
                finish(*waiting.pop(0), sends)
        for row, c in waiting:
            finish(row, c, sends)

    everything = [(r, c) for r in range(2) for c in range(chunks)]

    @pl.when(section == 0)
    def _():
        lend(1).start()
        for r in range(2):
            for far in range(1, heads):
                token_copy(r, far, head).start()
        time_copy.wait()
        cuts = (cut_0, cut_1)
        places = [
            (way[0][0], sum(count for _, count in way)) if way else None for way in q_spans
        ]
        for r in range(2):
            own_tokens[r].wait()
            for far in range(1, heads):
                token_copy(r, far, (head + heads - far) % heads).wait_recv()
            normed[...] = normalised(r)
            for way in range(2):
                if places[way] is not None:
                    begin, count = places[way]
                    for o in range(n):
                        cuts[way][o, r * PATCH : (r + 1) * PATCH, :] = normed[
                            :, o * q_rows + begin : o * q_rows + begin + count
                        ]

        tile = 768 if qkv_columns % 768 == 0 else qkv_columns

        def add_up(owner, way, start):
            if places[way] is None:
                return
            begin, count = places[way]

            def body(t, _):
                cols = (
                    pl.ds(pl.multiple_of(t * tile, 128), tile)
                    if tile < qkv_columns
                    else slice(None)
                )
                term = jnp.dot(
                    cuts[way][owner],
                    wq[owner, begin : begin + count, cols],
                    preferred_element_type=jnp.float32,
                )
                if start:
                    projected_all[:, cols] = term
                else:
                    projected_all[:, cols] += term
                return 0

            lax.fori_loop(0, qkv_columns // tile, body, 0)

        own[0].wait()
        for way in range(2):
            add_up(me, way, way == 0)

        def arrived(step):
            for way in range(2):
                owner = ring_index((place + (n - step if way == 0 else step)) % n, n)
                add_up(owner, way, False)

        lead = n // 8

        def q_step(step, _):
            relay(q_ring, step)

            @pl.when(step == lead)
            def _():
                begin_ring(part_ring)

            @pl.when(step > lead)
            def _():
                relay(part_ring, step - lead)

            spread(step - 1)
            arrived(step)
            return 0

        lax.fori_loop(1, n - 1, q_step, 0)
        own[1].wait()
        settle(q_ring)
        relay(part_ring, n - 1 - lead)
        arrived(n - 1)

        def project(r, j):
            begin = pl.ds(pl.multiple_of(r * PATCH, PATCH), PATCH)
            return projected_all[begin, columns_of(j)].astype(jnp.bfloat16)

        def beside(j):
            low = jnp.minimum(j * (lead - 1) // 2, lead - 1)
            high = jnp.minimum((j + 1) * (lead - 1) // 2, lead - 1)
            relays(part_ring, n - lead + low, n - lead + high)

        attend(0, project, beside)
        relays(part_ring, n - lead + jnp.minimum(groups * (lead - 1) // 2, lead - 1), n - 1)
        write_fresh(0).start()
        settle(part_ring)

        def back(step, _):
            for way, k in order_of(x_spans):
                give_back(step, way, k, 1).wait_recv()
            return 0

        lax.fori_loop(0, n - 1, back, 0)
        put_out([0], True, 2)
        write_hidden(0).start()
        attend(1, project, lambda j: None)
        write_fresh(1).start()
        put_out([1], True, 2)
        write_hidden(1).start()
        for r in range(2):
            for far in range(1, heads):
                token_copy(r, far, head).wait_send()
        for r, c in everything:
            onward(r, c, 1).wait_send()
        lend(1).wait_send()

    @pl.when(section == 1)
    def _():
        lend(0).wait_recv()
        begin_ring(x_ring)

        def hand_back(step):
            for way, k in order_of(x_spans):
                give_back(step, way, k, 0).start()

        def x_step(step):
            @pl.when(step < n - 1)
            def _():
                relay(x_ring, step)
                hand_back(step - 1)

            @pl.when(step == n - 1)
            def _():
                settle(x_ring)
                hand_back(n - 2)

        lead = n // 2
        q_first = [kind for kind in q_ring[1] if kind[1] == 0]
        q_rest = [kind for kind in q_ring[1] if kind[1] > 0]

        def q_step(step, _):
            x_step(2 * step - 1)
            relay((q_ring[0], q_first), step)
            x_step(2 * step)
            relay((q_ring[0], q_rest), step)

            @pl.when(step == lead)
            def _():
                begin_ring(whole_ring)

            @pl.when(step > lead)
            def _():
                relay(whole_ring, step - lead)

            spread(step - 1)
            return 0

        lax.fori_loop(1, n - 1, q_step, 0)
        own[1].wait()
        time_copy.wait()
        settle(q_ring)
        own[0].wait()
        early = n - lead
        relays(whole_ring, n - 1 - lead, early)

        def project(r, j):
            weight = wq[:, :, columns_of(j)].reshape(n * q_rows, span)
            return jnp.dot(normed[...], weight, preferred_element_type=jnp.float32).astype(
                jnp.bfloat16
            )

        def row_body(r, _):
            for c in range(chunks):
                onward(r, c, 0).wait_recv()
                for far in range(1, heads):
                    forward(r, c, far, head).start()
            for c in range(chunks):
                for far in range(1, heads):
                    forward(r, c, far, (head + heads - far) % heads).wait_recv()
            normed[...] = normalised(r)

            def beside(j):
                shift = groups * 2 // 3
                done = jnp.clip(r * groups + j - shift, 0, groups)
                later = jnp.clip(r * groups + j + 1 - shift, 0, groups)
                left_over = n - 1 - early
                relays(
                    whole_ring,
                    early + (done * left_over + groups - 1) // groups,
                    early + (later * left_over + groups - 1) // groups,
                )

            attend(r, project, beside)
            write_fresh(r).start()
            return 0

        lax.fori_loop(0, 2, row_body, 0)
        settle(whole_ring)
        put_out([0, 1], False, 4)
        for r in range(2):
            write_hidden(r).start()

        def handed(step, _):
            for way, k in order_of(x_spans):
                give_back(step, way, k, 0).wait_send()
            return 0

        lax.fori_loop(0, n - 1, handed, 0)
        for r, c in everything:
            for far in range(1, heads):
                forward(r, c, far, head).wait_send()

    for r, c in everything:
        for far in range(1, heads):
            share(r, c, far).wait_send()
    for r in range(2):
        write_fresh(r).wait()
        write_hidden(r).wait()


def shards(
    latent_tokens, w_qkv, w_out, time_mod, text_mod, stale_kv, guided, patch_index, timestep
):
    n = lax.axis_size("req")
    heads = lax.axis_size("head")
    rows, width = latent_tokens.shape[2:]
    columns = stale_kv.shape[-1]
    bf16, f32 = jnp.bfloat16, jnp.float32
    chunks = width // (384 if width % 384 == 0 else width)
    heads_here = columns // (2 * HD)
    group = 2 if heads_here % 2 == 0 else heads_here
    dma = pltpu.SemaphoreType.DMA
    smem = pl.BlockSpec(memory_space=pltpu.SMEM)
    vmem = pl.BlockSpec(memory_space=pltpu.VMEM)
    hbm = pl.BlockSpec(memory_space=pl.ANY)
    keys = PATCHES * PATCH
    lent = lent_rows(w_out.shape[2])
    counts = [sum(count for _, count in way) for way in cut(0, w_qkv.shape[1])]
    hidden, fresh = pl.pallas_call(
        functools.partial(fused_kernel, n, heads),
        out_shape=(
            jax.ShapeDtypeStruct((2, rows, width), bf16),
            jax.ShapeDtypeStruct((2, PATCH, columns), bf16),
        ),
        in_specs=[smem, smem, smem, hbm, hbm, hbm, hbm, vmem, hbm],
        out_specs=[hbm, hbm],
        scratch_shapes=[
            pltpu.VMEM((2, rows, width), bf16),
            pltpu.VMEM((2, PATCH, columns), bf16),
            pltpu.VMEM((time_mod.shape[1], time_mod.shape[2], 1, width), f32),
            pltpu.VMEM((n, *w_qkv.shape[1:]), bf16),
            pltpu.VMEM((n, w_out.shape[2], w_out.shape[1]), bf16),
            pltpu.VMEM((n, lent, w_out.shape[1]), bf16),
            pltpu.VMEM((STALE, 2, columns), bf16),
            pltpu.VMEM((2, keys, columns), bf16),
            pltpu.VMEM((2, keys, columns), bf16),
            pltpu.VMEM((2, PATCH, width), bf16),
            pltpu.VMEM((PATCH, width), bf16),
            *[pltpu.VMEM((n, 2 * PATCH, max(16, count)), bf16) for count in counts],
            pltpu.VMEM((2 * PATCH, w_qkv.shape[2]), f32),
            pltpu.VMEM((2, PATCH, columns // 2), bf16),
            pltpu.VMEM((2, PATCH, keys + PATCH), f32),
            pltpu.VMEM((2, PATCH, 128), f32),
            pltpu.VMEM((PATCH, group * 3 * HD), bf16),
            pltpu.VMEM((2, PATCH, width), bf16),
            pltpu.VMEM((heads - 1, 2, rows, width), bf16),
            pltpu.VMEM((2, rows, width), bf16),
            dma((2, 2)),
            dma((n - 1, 2, 2)),
            dma((2, 2)),
            dma((n - 1, 2, 2)),
            dma((2, 2)),
            dma((n - 1, 2, 2)),
            dma((n - 1, 2, 2)),
            dma((n - 1, 2, 2)),
            dma((2,)),
            dma((10,)),
            dma((2, heads - 1)),
            dma((2, heads - 1)),
            dma((2, chunks, heads - 1)),
            dma((2, chunks, heads - 1)),
            dma((2, chunks)),
            dma((2, chunks)),
            dma((2, chunks, heads - 1)),
            dma((2, chunks, heads - 1)),
        ],
        compiler_params=pltpu.CompilerParams(
            collective_id=0, has_side_effects=True, vmem_limit_bytes=58 << 20
        ),
    )(
        timestep,
        patch_index,
        guided,
        latent_tokens[0],
        w_qkv[0],
        w_out[0].T,
        jnp.transpose(time_mod, (1, 2, 0, 3)),
        jnp.swapaxes(text_mod[0, 0], 0, 1),
        jnp.swapaxes(stale_kv[0, 0], 0, 1),
    )
    return (hidden[None, None], fresh[None, None])


def solution(mesh):
    in_specs = (
        P("req", None, "head", None),
        P("section", "req", "head"),
        P("section", "head", "req"),
        P("section", None, None, None),
        P("section", "req", None, None, None),
        P("section", "req", None, None, "head"),
        P("req"),
        P("req"),
        P("req"),
    )
    out_specs = (P("section", "req", None, "head", None), P("section", "req", None, None, "head"))
    return jax.shard_map(shards, mesh=mesh, in_specs=in_specs, out_specs=out_specs, check_vma=False)
```

```python
import functools

import jax
import jax.numpy as jnp
from jax import lax
from jax.experimental import pallas as pl
from jax.experimental.pallas import tpu as pltpu
from jax.sharding import PartitionSpec as P

HD = 64
PATCH = 256
PATCHES = 4
STALE = 1178
TEXT = STALE - PATCHES * PATCH
MESH = pl.DeviceIdType.MESH


def ring_index(place, n):
    return jnp.where(place < n // 2, 2 * place, 2 * (n - 1 - place) + 1)


def nt_dot(a, b):
    return lax.dot_general(a, b, (((1,), (1,)), ((), ())), preferred_element_type=jnp.float32)


def cut(begin, rows):
    unit = 16
    units = rows // unit
    first = (units + 1) // 2
    ways = []
    for start, count in ((0, first), (first, units - first)):
        head = (count + 1) // 2
        spans = []
        if head > 0:
            spans.append((begin + start * unit, head * unit))
        if count > head:
            spans.append((begin + (start + head) * unit, (count - head) * unit))
        ways.append(spans)
    return ways


def order_of(spans):
    most = max(len(way) for way in spans)
    return [(way, k) for k in range(most) for way in range(2) if k < len(spans[way])]


def heads_a_step(heads_here):
    return next(k for k in (4, 2, heads_here) if heads_here % k == 0)


def lent_rows(rows):
    return rows * 2 // 3 // 16 * 16


def fused_kernel(
    n,
    heads,
    timestep,
    patch,
    guided,
    tokens,
    wq_in,
    wo_in,
    time_in,
    text_mod,
    stale,
    hidden_to,
    fresh_to,
    hidden_out,
    fresh_out,
    time_mod,
    wq,
    wo,
    wx,
    raw,
    kv,
    ve,
    hbuf,
    normed,
    cut_0,
    cut_1,
    projected_all,
    mixed,
    scores,
    tops,
    pscr,
    terms,
    inbox,
    mine,
    q_send,
    q_recv,
    o_send,
    o_recv,
    w_send,
    w_recv,
    l_send,
    l_recv,
    g_sem,
    own_sem,
    t_send,
    t_recv,
    e_send,
    e_recv,
    x_send,
    x_recv,
    f_send,
    f_recv,
):
    me = lax.axis_index("req")
    head = lax.axis_index("head")
    section = lax.axis_index("section")
    place = jnp.where(me % 2 == 0, me // 2, n - 1 - me // 2)
    right = ring_index((place + 1) % n, n)
    left = ring_index((place + n - 1) % n, n)
    width = hbuf.shape[-1]
    rows = PATCH // heads
    heads_here = kv.shape[-1] // (2 * HD)
    group = heads_a_step(heads_here)
    groups = heads_here // group
    chunk = 384 if width % 384 == 0 else width
    chunks = width // chunk
    q_rows, o_rows = wq_in.shape[0], wo_in.shape[0]
    lent = lent_rows(o_rows)
    kept_rows = o_rows - lent
    span = group * 3 * HD
    qkv_columns = wq_in.shape[1]

    own = [
        pltpu.make_async_copy(wq_in, wq.at[me], own_sem.at[0]),
        pltpu.make_async_copy(wo_in, wo.at[me], own_sem.at[1]),
        pltpu.make_async_copy(stale, raw, own_sem.at[2]),
    ]
    own_rows = pl.ds(pl.multiple_of(head * rows, rows), rows)
    time_copy = pltpu.make_async_copy(time_in, time_mod, own_sem.at[5])
    time_copy.start()

    def write_hidden(r):
        return pltpu.make_async_copy(hidden_out.at[r], hidden_to.at[r], own_sem.at[6 + r])

    def write_fresh(r):
        return pltpu.make_async_copy(fresh_out.at[r], fresh_to.at[r], own_sem.at[8 + r])

    own_tokens = [
        pltpu.make_async_copy(tokens.at[r], hbuf.at[r, own_rows], own_sem.at[3 + r])
        for r in range(2)
    ]

    barrier = pltpu.get_barrier_semaphore()
    for neighbour in (left, right):
        pl.semaphore_signal(barrier, inc=1, device_id={"req": neighbour}, device_id_type=MESH)
    for far in range(1, heads):
        peer = {"head": (head + far) % heads}
        pl.semaphore_signal(barrier, inc=1, device_id=peer, device_id_type=MESH)
    pl.semaphore_signal(barrier, inc=1, device_id={"section": 1 - section}, device_id_type=MESH)

    @pl.when(section == 0)
    def _():
        for copy in own_tokens:
            copy.start()

    for copy in own:
        copy.start()
    pl.semaphore_wait(barrier, 2 + heads)

    def hop(source, target, spans, shift, send, recv, step, way, number, first=False):
        begin, count = spans[way][number]
        owner = ring_index((place + (n - step if way == 0 else step)) % n, n)
        into = pl.ds(begin, count)
        return pltpu.make_async_remote_copy(
            src_ref=source.at[into] if first else target.at[owner, into],
            dst_ref=target.at[owner, into],
            send_sem=send.at[way, number],
            recv_sem=recv.at[step, way, number],
            device_id={"req": right if way == 0 else left},
            device_id_type=MESH,
        )

    def ring(source, target, spans, send, recv):
        return functools.partial(hop, source, target, spans, 0, send, recv), order_of(spans)

    q_spans = cut(0, q_rows)
    x_spans = cut(0, lent)
    q_ring = ring(wq_in, wq, q_spans, q_send, q_recv)
    part_ring = ring(wo_in, wo, cut(0, kept_rows), o_send, o_recv)
    whole_ring = ring(wo_in, wo, cut(0, o_rows), o_send, o_recv)
    x_ring = ring(wx.at[me], wx, x_spans, w_send, w_recv)

    def begin_ring(made):
        for way, k in made[1]:
            made[0](0, way, k, first=True).start()

    def relay(made, step):
        for way, k in made[1]:
            before = made[0](step - 1, way, k)
            before.wait_recv()
            before.wait_send()
            made[0](step, way, k).start()

    def relays(made, low, high):
        lax.fori_loop(low, high, lambda s, _: (relay(made, s), 0)[1], 0)

    def settle(made):
        for way, k in made[1]:
            last = made[0](n - 2, way, k)
            last.wait_recv()
            last.wait_send()

    def lend(target):
        return pltpu.make_async_remote_copy(
            src_ref=wo_in.at[pl.ds(kept_rows, lent)],
            dst_ref=wx.at[me],
            send_sem=g_sem.at[0],
            recv_sem=g_sem.at[1],
            device_id={"section": target},
            device_id_type=MESH,
        )

    def give_back(step, way, number, target):
        begin, count = x_spans[way][number]
        owner = ring_index((place + (n - 1 - step if way == 0 else step + 1)) % n, n)
        return pltpu.make_async_remote_copy(
            src_ref=wx.at[owner, pl.ds(begin, count)],
            dst_ref=wo.at[owner, pl.ds(kept_rows + begin, count)],
            send_sem=l_send.at[step, way, number],
            recv_sem=l_recv.at[step, way, number],
            device_id={"section": target},
            device_id_type=MESH,
        )

    def token_copy(r, far, owner):
        into = pl.ds(pl.multiple_of(owner * rows, rows), rows)
        return pltpu.make_async_remote_copy(
            src_ref=tokens.at[r],
            dst_ref=hbuf.at[r, into],
            send_sem=t_send.at[r, far - 1],
            recv_sem=t_recv.at[r, far - 1],
            device_id={"head": (head + far) % heads},
            device_id_type=MESH,
        )

    begin_ring(q_ring)

    patch_here = patch[0]
    lane2 = lax.broadcasted_iota(jnp.int32, (2, 1, 2 * HD), 2)
    text_pad = TEXT // 16 * 16

    def spread(block):
        @pl.when(block == 0)
        def _():
            own[2].wait()
            zero = jnp.zeros((2, PATCH - text_pad, kv.shape[-1]), kv.dtype)
            kv[:, (PATCHES - 1) * PATCH + text_pad :, :] = zero
            ve[:, (PATCHES - 1) * PATCH + text_pad :, :] = zero

        def lanes_of(c):
            return pl.ds(pl.multiple_of(c * 2 * HD, 2 * HD), 2 * HD)

        @pl.when(block < PATCHES - 1)
        def _():
            begin = (block + (block >= patch_here).astype(jnp.int32)) * PATCH
            into = pl.ds(pl.multiple_of(block * PATCH, PATCH), PATCH)

            def body(c, _):
                pair = jnp.swapaxes(raw[pl.ds(begin, PATCH), :, lanes_of(c)], 0, 1)
                kv[:, into, lanes_of(c)] = pair
                ve[:, into, lanes_of(c)] = jnp.where(lane2 < HD, jnp.bfloat16(1), pair)
                return 0

            lax.fori_loop(0, heads_here, body, 0)

        @pl.when(block == PATCHES - 1)
        def _():
            first = (PATCHES - 1) * PATCH

            def body(c, _):
                pair = jnp.swapaxes(raw[PATCHES * PATCH :, :, lanes_of(c)], 0, 1)
                kv[:, first : first + TEXT, lanes_of(c)] = pair
                ve[:, first : first + TEXT, lanes_of(c)] = jnp.where(
                    lane2 < HD, jnp.bfloat16(1), pair
                )
                return 0

            lax.fori_loop(0, heads_here, body, 0)

    time_here = timestep[0]

    def modulation(k, r):
        return time_mod[time_here, k] + text_mod[k, pl.ds(r, 1), :]

    def normalised(r):
        values_f = hbuf[r].astype(jnp.float32)
        row_mean = jnp.mean(values_f, axis=-1, keepdims=True)
        centered = values_f - row_mean
        row_var = jnp.mean(centered * centered, axis=-1, keepdims=True)
        scaled = centered * lax.rsqrt(row_var + 1e-06)
        return (scaled * (1.0 + modulation(1, r)) + modulation(0, r)).astype(jnp.bfloat16)

    def onward(r, c, target):
        lanes = pl.ds(c * chunk, chunk)
        return pltpu.make_async_remote_copy(
            src_ref=mine.at[r, :, lanes],
            dst_ref=hbuf.at[r, own_rows, lanes],
            send_sem=x_send.at[r, c],
            recv_sem=x_recv.at[r, c],
            device_id={"section": target},
            device_id_type=MESH,
        )

    def forward(r, c, far, owner):
        into = pl.ds(pl.multiple_of(owner * rows, rows), rows)
        lanes = pl.ds(c * chunk, chunk)
        return pltpu.make_async_remote_copy(
            src_ref=hbuf.at[r, into, lanes],
            dst_ref=hbuf.at[r, into, lanes],
            send_sem=f_send.at[r, c, far - 1],
            recv_sem=f_recv.at[r, c, far - 1],
            device_id={"head": (head + far) % heads},
            device_id_type=MESH,
        )

    keep = [jnp.float32(1.0), (guided[0] != 0).astype(jnp.float32)]
    lane = lax.broadcasted_iota(jnp.int32, (PATCH, PATCH), 1)
    lane1 = lax.broadcasted_iota(jnp.int32, (PATCH, 2 * HD), 1)
    blank = jnp.zeros((PATCH, HD), jnp.bfloat16)

    def columns_of(j):
        return pl.ds(pl.multiple_of(j * span, 128), span) if groups > 1 else slice(None)

    def lanes_of(j, h):
        return pl.ds(pl.multiple_of((j * group + h) * 2 * HD, 2 * HD), 2 * HD)

    def score(r, j, h, projected, slot):
        query = projected[:, h * 3 * HD : h * 3 * HD + HD]
        pair = projected[:, h * 3 * HD + HD : (h + 1) * 3 * HD]
        query = jnp.concatenate([query * jnp.bfloat16(HD**-0.5), blank], axis=1)
        most = None
        for b in range(PATCHES + 1):
            part = pair if b == 0 else kv[r, (b - 1) * PATCH : b * PATCH, lanes_of(j, h)]
            block = nt_dot(query, part)
            if b == PATCHES:
                block = jnp.where(lane < TEXT, block, -jnp.inf)
            scores[slot, :, b * PATCH : (b + 1) * PATCH] = block
            here = jnp.maximum(block[:, :128], block[:, 128:])
            most = here if most is None else jnp.maximum(most, here)
        tops[slot] = jnp.broadcast_to(jnp.max(most, axis=-1, keepdims=True), (PATCH, 128))

    def mix(r, j, h, projected, slot):
        keep_here = jnp.where(r == 0, keep[0], keep[1])
        pair = projected[:, h * 3 * HD + HD : (h + 1) * 3 * HD]
        fresh_out[r, :, lanes_of(j, h)] = (pair.astype(jnp.float32) * keep_here).astype(
            jnp.bfloat16
        )
        top = tops[slot]
        top = jnp.concatenate([top, top], axis=1)
        total = None
        for b in range(PATCHES + 1):
            if b == 0:
                value = jnp.where(lane1 < HD, jnp.bfloat16(1), pair)
            else:
                value = ve[r, (b - 1) * PATCH : b * PATCH, lanes_of(j, h)]
            weight = jnp.exp(scores[slot, :, b * PATCH : (b + 1) * PATCH] - top)
            term = jnp.dot(weight.astype(jnp.bfloat16), value, preferred_element_type=jnp.float32)
            total = term if total is None else total + term
        return (total[:, HD:] / total[:, :HD]).astype(jnp.bfloat16)

    def attend(r, project, beside):
        first = project(r, 0)
        pscr[...] = first
        score(r, 0, 0, first, 0)

        def group_body(j, _):
            beside(j)
            projected = pscr[...]
            outs = []
            if groups > 1:
                following = jnp.minimum(j + 1, groups - 1)
                later = project(r, following)
            for h in range(group):
                if h + 1 < group:
                    score(r, j, h + 1, projected, (h + 1) % 2)
                elif groups > 1:
                    score(r, following, 0, later, 0)
                outs.append(mix(r, j, h, projected, h % 2))
            if groups > 1:
                pscr[...] = later
                cols = pl.ds(pl.multiple_of(j * group * HD, 128), group * HD)
            else:
                cols = slice(None)
            mixed[r, :, cols] = jnp.concatenate(outs, axis=1)
            return 0

        lax.fori_loop(0, groups, group_body, 0)

    def share(r, c, far):
        peer = (head + far) % heads
        lanes = pl.ds(c * chunk, chunk)
        return pltpu.make_async_remote_copy(
            src_ref=terms.at[r, pl.ds(pl.multiple_of(peer * rows, rows), rows), lanes],
            dst_ref=inbox.at[far - 1, r, :, lanes],
            send_sem=e_send.at[r, c, far - 1],
            recv_sem=e_recv.at[r, c, far - 1],
            device_id={"head": peer},
            device_id_type=MESH,
        )

    def finish(r, c, sends):
        lanes = slice(c * chunk, (c + 1) * chunk)
        attn = terms[r, own_rows, lanes].astype(jnp.float32)
        for far in range(1, heads):
            share(r, c, far).wait_recv()
            attn = attn + inbox[far - 1, r, :, lanes].astype(jnp.float32)
        before = hbuf[r, own_rows, lanes].astype(jnp.float32)
        gate = modulation(2, r)[:, lanes]
        updated = (before + gate * attn).astype(jnp.bfloat16)
        hidden_out[r, :, lanes] = (updated.astype(jnp.float32) * keep[r]).astype(jnp.bfloat16)
        if sends:
            mine[r, :, lanes] = updated
            onward(r, c, 1).start()

    blocks = chunk // o_rows

    def put_out(some_rows, sends, lag):
        steps = [(r, c) for r in some_rows for c in range(chunks)]
        if len(some_rows) == 2:
            steps = [(None, c) for c in range(chunks)]
        waiting = []
        for r, c in steps:
            lanes = slice(c * chunk, (c + 1) * chunk)
            weight = wo[c * blocks : (c + 1) * blocks].reshape(chunk, wo.shape[2])
            if r is None:
                both = mixed[...].reshape(2 * PATCH, wo.shape[2])
                term = nt_dot(both, weight).astype(jnp.bfloat16)
                terms[:, :, lanes] = term.reshape(2, PATCH, chunk)
            else:
                terms[r, :, lanes] = nt_dot(mixed[r], weight).astype(jnp.bfloat16)
            for row in range(2) if r is None else [r]:
                for far in range(1, heads):
                    share(row, c, far).start()
                waiting.append((row, c))
            while len(waiting) > lag:
                finish(*waiting.pop(0), sends)
        for row, c in waiting:
            finish(row, c, sends)

    everything = [(r, c) for r in range(2) for c in range(chunks)]

    @pl.when(section == 0)
    def _():
        lend(1).start()
        for r in range(2):
            for far in range(1, heads):
                token_copy(r, far, head).start()
        time_copy.wait()
        cuts = (cut_0, cut_1)
        places = [
            (way[0][0], sum(count for _, count in way)) if way else None for way in q_spans
        ]
        for r in range(2):
            own_tokens[r].wait()
            for far in range(1, heads):
                token_copy(r, far, (head + heads - far) % heads).wait_recv()
            normed[...] = normalised(r)
            for way in range(2):
                if places[way] is not None:
                    begin, count = places[way]
                    for o in range(n):
                        cuts[way][o, r * PATCH : (r + 1) * PATCH, :] = normed[
                            :, o * q_rows + begin : o * q_rows + begin + count
                        ]

        tile = 768 if qkv_columns % 768 == 0 else qkv_columns

        def add_up(owner, way, start):
            if places[way] is None:
                return
            begin, count = places[way]

            def body(t, _):
                cols = (
                    pl.ds(pl.multiple_of(t * tile, 128), tile)
                    if tile < qkv_columns
                    else slice(None)
                )
                term = jnp.dot(
                    cuts[way][owner],
                    wq[owner, begin : begin + count, cols],
                    preferred_element_type=jnp.float32,
                )
                if start:
                    projected_all[:, cols] = term
                else:
                    projected_all[:, cols] += term
                return 0

            lax.fori_loop(0, qkv_columns // tile, body, 0)

        own[0].wait()
        for way in range(2):
            add_up(me, way, way == 0)

        def arrived(step):
            for way in range(2):
                owner = ring_index((place + (n - step if way == 0 else step)) % n, n)
                add_up(owner, way, False)

        lead = n // 8

        def q_step(step, _):
            relay(q_ring, step)

            @pl.when(step == lead)
            def _():
                begin_ring(part_ring)

            @pl.when(step > lead)
            def _():
                relay(part_ring, step - lead)

            spread(step - 1)
            arrived(step)
            return 0

        lax.fori_loop(1, n - 1, q_step, 0)
        own[1].wait()
        settle(q_ring)
        relay(part_ring, n - 1 - lead)
        arrived(n - 1)

        def project(r, j):
            begin = pl.ds(pl.multiple_of(r * PATCH, PATCH), PATCH)
            return projected_all[begin, columns_of(j)].astype(jnp.bfloat16)

        def beside(j):
            low = jnp.minimum(j * (lead - 1) // 2, lead - 1)
            high = jnp.minimum((j + 1) * (lead - 1) // 2, lead - 1)
            relays(part_ring, n - lead + low, n - lead + high)

        attend(0, project, beside)
        relays(part_ring, n - lead + jnp.minimum(groups * (lead - 1) // 2, lead - 1), n - 1)
        write_fresh(0).start()
        settle(part_ring)

        def back(step, _):
            for way, k in order_of(x_spans):
                give_back(step, way, k, 1).wait_recv()
            return 0

        lax.fori_loop(0, n - 1, back, 0)
        put_out([0], True, 2)
        write_hidden(0).start()
        attend(1, project, lambda j: None)
        write_fresh(1).start()
        put_out([1], True, 2)
        write_hidden(1).start()
        for r in range(2):
            for far in range(1, heads):
                token_copy(r, far, head).wait_send()
        for r, c in everything:
            onward(r, c, 1).wait_send()
        lend(1).wait_send()

    @pl.when(section == 1)
    def _():
        lend(0).wait_recv()
        begin_ring(x_ring)

        def hand_back(step):
            for way, k in order_of(x_spans):
                give_back(step, way, k, 0).start()

        def x_step(step):
            @pl.when(step < n - 1)
            def _():
                relay(x_ring, step)
                hand_back(step - 1)

            @pl.when(step == n - 1)
            def _():
                settle(x_ring)
                hand_back(n - 2)

        lead = n // 2
        q_first = [kind for kind in q_ring[1] if kind[1] == 0]
        q_rest = [kind for kind in q_ring[1] if kind[1] > 0]

        def q_step(step, _):
            x_step(2 * step - 1)
            relay((q_ring[0], q_first), step)
            x_step(2 * step)
            relay((q_ring[0], q_rest), step)

            @pl.when(step == lead)
            def _():
                begin_ring(whole_ring)

            @pl.when(step > lead)
            def _():
                relay(whole_ring, step - lead)

            spread(step - 1)
            return 0

        lax.fori_loop(1, n - 1, q_step, 0)
        own[1].wait()
        time_copy.wait()
        settle(q_ring)
        own[0].wait()
        early = n - lead
        relays(whole_ring, n - 1 - lead, early)

        def project(r, j):
            weight = wq[:, :, columns_of(j)].reshape(n * q_rows, span)
            return jnp.dot(normed[...], weight, preferred_element_type=jnp.float32).astype(
                jnp.bfloat16
            )

        def row_body(r, _):
            for c in range(chunks):
                onward(r, c, 0).wait_recv()
                for far in range(1, heads):
                    forward(r, c, far, head).start()
            for c in range(chunks):
                for far in range(1, heads):
                    forward(r, c, far, (head + heads - far) % heads).wait_recv()
            normed[...] = normalised(r)

            def beside(j):
                shift = groups * 2 // 3
                done = jnp.clip(r * groups + j - shift, 0, groups)
                later = jnp.clip(r * groups + j + 1 - shift, 0, groups)
                left_over = n - 1 - early
                relays(
                    whole_ring,
                    early + (done * left_over + groups - 1) // groups,
                    early + (later * left_over + groups - 1) // groups,
                )

            attend(r, project, beside)
            write_fresh(r).start()
            return 0

        lax.fori_loop(0, 2, row_body, 0)
        settle(whole_ring)
        put_out([0, 1], False, 4)
        for r in range(2):
            write_hidden(r).start()

        def handed(step, _):
            for way, k in order_of(x_spans):
                give_back(step, way, k, 0).wait_send()
            return 0

        lax.fori_loop(0, n - 1, handed, 0)
        for r, c in everything:
            for far in range(1, heads):
                forward(r, c, far, head).wait_send()

    for r, c in everything:
        for far in range(1, heads):
            share(r, c, far).wait_send()
    for r in range(2):
        write_fresh(r).wait()
        write_hidden(r).wait()


def shards(
    latent_tokens, w_qkv, w_out, time_mod, text_mod, stale_kv, guided, patch_index, timestep
):
    n = lax.axis_size("req")
    heads = lax.axis_size("head")
    rows, width = latent_tokens.shape[2:]
    columns = stale_kv.shape[-1]
    bf16, f32 = jnp.bfloat16, jnp.float32
    chunks = width // (384 if width % 384 == 0 else width)
    heads_here = columns // (2 * HD)
    group = heads_a_step(heads_here)
    dma = pltpu.SemaphoreType.DMA
    smem = pl.BlockSpec(memory_space=pltpu.SMEM)
    vmem = pl.BlockSpec(memory_space=pltpu.VMEM)
    hbm = pl.BlockSpec(memory_space=pl.ANY)
    keys = PATCHES * PATCH
    lent = lent_rows(w_out.shape[2])
    counts = [sum(count for _, count in way) for way in cut(0, w_qkv.shape[1])]
    hidden, fresh = pl.pallas_call(
        functools.partial(fused_kernel, n, heads),
        out_shape=(
            jax.ShapeDtypeStruct((2, rows, width), bf16),
            jax.ShapeDtypeStruct((2, PATCH, columns), bf16),
        ),
        in_specs=[smem, smem, smem, hbm, hbm, hbm, hbm, vmem, hbm],
        out_specs=[hbm, hbm],
        scratch_shapes=[
            pltpu.VMEM((2, rows, width), bf16),
            pltpu.VMEM((2, PATCH, columns), bf16),
            pltpu.VMEM((time_mod.shape[1], time_mod.shape[2], 1, width), f32),
            pltpu.VMEM((n, *w_qkv.shape[1:]), bf16),
            pltpu.VMEM((n, w_out.shape[2], w_out.shape[1]), bf16),
            pltpu.VMEM((n, lent, w_out.shape[1]), bf16),
            pltpu.VMEM((STALE, 2, columns), bf16),
            pltpu.VMEM((2, keys, columns), bf16),
            pltpu.VMEM((2, keys, columns), bf16),
            pltpu.VMEM((2, PATCH, width), bf16),
            pltpu.VMEM((PATCH, width), bf16),
            *[pltpu.VMEM((n, 2 * PATCH, max(16, count)), bf16) for count in counts],
            pltpu.VMEM((2 * PATCH, w_qkv.shape[2]), f32),
            pltpu.VMEM((2, PATCH, columns // 2), bf16),
            pltpu.VMEM((2, PATCH, keys + PATCH), f32),
            pltpu.VMEM((2, PATCH, 128), f32),
            pltpu.VMEM((PATCH, group * 3 * HD), bf16),
            pltpu.VMEM((2, PATCH, width), bf16),
            pltpu.VMEM((heads - 1, 2, rows, width), bf16),
            pltpu.VMEM((2, rows, width), bf16),
            dma((2, 2)),
            dma((n - 1, 2, 2)),
            dma((2, 2)),
            dma((n - 1, 2, 2)),
            dma((2, 2)),
            dma((n - 1, 2, 2)),
            dma((n - 1, 2, 2)),
            dma((n - 1, 2, 2)),
            dma((2,)),
            dma((10,)),
            dma((2, heads - 1)),
            dma((2, heads - 1)),
            dma((2, chunks, heads - 1)),
            dma((2, chunks, heads - 1)),
            dma((2, chunks)),
            dma((2, chunks)),
            dma((2, chunks, heads - 1)),
            dma((2, chunks, heads - 1)),
        ],
        compiler_params=pltpu.CompilerParams(
            collective_id=0, has_side_effects=True, vmem_limit_bytes=58 << 20
        ),
    )(
        timestep,
        patch_index,
        guided,
        latent_tokens[0],
        w_qkv[0],
        w_out[0].T,
        jnp.transpose(time_mod, (1, 2, 0, 3)),
        jnp.swapaxes(text_mod[0, 0], 0, 1),
        jnp.swapaxes(stale_kv[0, 0], 0, 1),
    )
    return (hidden[None, None], fresh[None, None])


def solution(mesh):
    in_specs = (
        P("req", None, "head", None),
        P("section", "req", "head"),
        P("section", "head", "req"),
        P("section", None, None, None),
        P("section", "req", None, None, None),
        P("section", "req", None, None, "head"),
        P("req"),
        P("req"),
        P("req"),
    )
    out_specs = (P("section", "req", None, "head", None), P("section", "req", None, None, "head"))
    return jax.shard_map(shards, mesh=mesh, in_specs=in_specs, out_specs=out_specs, check_vma=False)
```

```python
import functools

import jax
import jax.numpy as jnp
from jax import lax
from jax.experimental import pallas as pl
from jax.experimental.pallas import tpu as pltpu
from jax.sharding import PartitionSpec as P

HD = 64
PATCH = 256
PATCHES = 4
STALE = 1178
TEXT = STALE - PATCHES * PATCH
MESH = pl.DeviceIdType.MESH


def ring_index(place, n):
    return jnp.where(place < n // 2, 2 * place, 2 * (n - 1 - place) + 1)


def nt_dot(a, b):
    return lax.dot_general(a, b, (((1,), (1,)), ((), ())), preferred_element_type=jnp.float32)


def cut(begin, rows):
    unit = 16
    units = rows // unit
    first = (units + 1) // 2
    ways = []
    for start, count in ((0, first), (first, units - first)):
        head = (count + 1) // 2
        spans = []
        if head > 0:
            spans.append((begin + start * unit, head * unit))
        if count > head:
            spans.append((begin + (start + head) * unit, (count - head) * unit))
        ways.append(spans)
    return ways


def order_of(spans):
    most = max(len(way) for way in spans)
    return [(way, k) for k in range(most) for way in range(2) if k < len(spans[way])]


def heads_a_step(heads_here):
    return next(k for k in (4, 2, heads_here) if heads_here % k == 0)


def lent_rows(rows):
    return rows * 2 // 3 // 16 * 16


def fused_kernel(
    n,
    heads,
    timestep,
    patch,
    guided,
    tokens,
    wq_in,
    wo_in,
    time_in,
    text_mod,
    stale,
    hidden_to,
    fresh_to,
    hidden_out,
    fresh_out,
    time_mod,
    wq,
    wo,
    wx,
    raw,
    kv,
    ve,
    hbuf,
    normed,
    cut_0,
    cut_1,
    projected_all,
    mixed,
    scores,
    tops,
    pscr,
    terms,
    inbox,
    mine,
    q_send,
    q_recv,
    o_send,
    o_recv,
    w_send,
    w_recv,
    l_send,
    l_recv,
    g_sem,
    own_sem,
    t_send,
    t_recv,
    e_send,
    e_recv,
    x_send,
    x_recv,
    f_send,
    f_recv,
):
    me = lax.axis_index("req")
    head = lax.axis_index("head")
    section = lax.axis_index("section")
    place = jnp.where(me % 2 == 0, me // 2, n - 1 - me // 2)
    right = ring_index((place + 1) % n, n)
    left = ring_index((place + n - 1) % n, n)
    width = hbuf.shape[-1]
    rows = PATCH // heads
    heads_here = kv.shape[-1] // (2 * HD)
    group = heads_a_step(heads_here)
    groups = heads_here // group
    chunk = 384 if width % 384 == 0 else width
    chunks = width // chunk
    q_rows, o_rows = wq_in.shape[0], wo_in.shape[0]
    lent = lent_rows(o_rows)
    kept_rows = o_rows - lent
    span = group * 3 * HD
    qkv_columns = wq_in.shape[1]

    own = [
        pltpu.make_async_copy(wq_in, wq.at[me], own_sem.at[0]),
        pltpu.make_async_copy(wo_in, wo.at[me], own_sem.at[1]),
        pltpu.make_async_copy(stale, raw, own_sem.at[2]),
    ]
    own_rows = pl.ds(pl.multiple_of(head * rows, rows), rows)
    time_copy = pltpu.make_async_copy(time_in, time_mod, own_sem.at[5])
    time_copy.start()

    def write_hidden(r):
        return pltpu.make_async_copy(hidden_out.at[r], hidden_to.at[r], own_sem.at[6 + r])

    def write_fresh(r):
        return pltpu.make_async_copy(fresh_out.at[r], fresh_to.at[r], own_sem.at[8 + r])

    own_tokens = [
        pltpu.make_async_copy(tokens.at[r], hbuf.at[r, own_rows], own_sem.at[3 + r])
        for r in range(2)
    ]

    barrier = pltpu.get_barrier_semaphore()
    for neighbour in (left, right):
        pl.semaphore_signal(barrier, inc=1, device_id={"req": neighbour}, device_id_type=MESH)
    for far in range(1, heads):
        peer = {"head": (head + far) % heads}
        pl.semaphore_signal(barrier, inc=1, device_id=peer, device_id_type=MESH)
    pl.semaphore_signal(barrier, inc=1, device_id={"section": 1 - section}, device_id_type=MESH)

    @pl.when(section == 0)
    def _():
        for copy in own_tokens:
            copy.start()

    for copy in own:
        copy.start()
    pl.semaphore_wait(barrier, 2 + heads)

    def hop(source, target, spans, shift, send, recv, step, way, number, first=False):
        begin, count = spans[way][number]
        owner = ring_index((place + (n - step if way == 0 else step)) % n, n)
        into = pl.ds(begin, count)
        return pltpu.make_async_remote_copy(
            src_ref=source.at[into] if first else target.at[owner, into],
            dst_ref=target.at[owner, into],
            send_sem=send.at[way, number],
            recv_sem=recv.at[step, way, number],
            device_id={"req": right if way == 0 else left},
            device_id_type=MESH,
        )

    def ring(source, target, spans, send, recv):
        return functools.partial(hop, source, target, spans, 0, send, recv), order_of(spans)

    q_spans = cut(0, q_rows)
    x_spans = cut(0, lent)
    q_ring = ring(wq_in, wq, q_spans, q_send, q_recv)
    part_ring = ring(wo_in, wo, cut(0, kept_rows), o_send, o_recv)
    whole_ring = ring(wo_in, wo, cut(0, o_rows), o_send, o_recv)
    x_ring = ring(wx.at[me], wx, x_spans, w_send, w_recv)

    def begin_ring(made):
        for way, k in made[1]:
            made[0](0, way, k, first=True).start()

    def relay(made, step):
        for way, k in made[1]:
            before = made[0](step - 1, way, k)
            before.wait_recv()
            before.wait_send()
            made[0](step, way, k).start()

    def relays(made, low, high):
        lax.fori_loop(low, high, lambda s, _: (relay(made, s), 0)[1], 0)

    def settle(made):
        for way, k in made[1]:
            last = made[0](n - 2, way, k)
            last.wait_recv()
            last.wait_send()

    def lend(target):
        return pltpu.make_async_remote_copy(
            src_ref=wo_in.at[pl.ds(kept_rows, lent)],
            dst_ref=wx.at[me],
            send_sem=g_sem.at[0],
            recv_sem=g_sem.at[1],
            device_id={"section": target},
            device_id_type=MESH,
        )

    def give_back(step, way, number, target):
        begin, count = x_spans[way][number]
        owner = ring_index((place + (n - 1 - step if way == 0 else step + 1)) % n, n)
        return pltpu.make_async_remote_copy(
            src_ref=wx.at[owner, pl.ds(begin, count)],
            dst_ref=wo.at[owner, pl.ds(kept_rows + begin, count)],
            send_sem=l_send.at[step, way, number],
            recv_sem=l_recv.at[step, way, number],
            device_id={"section": target},
            device_id_type=MESH,
        )

    def token_copy(r, far, owner):
        into = pl.ds(pl.multiple_of(owner * rows, rows), rows)
        return pltpu.make_async_remote_copy(
            src_ref=tokens.at[r],
            dst_ref=hbuf.at[r, into],
            send_sem=t_send.at[r, far - 1],
            recv_sem=t_recv.at[r, far - 1],
            device_id={"head": (head + far) % heads},
            device_id_type=MESH,
        )

    begin_ring(q_ring)

    patch_here = patch[0]
    lane2 = lax.broadcasted_iota(jnp.int32, (2, 1, 2 * HD), 2)
    text_pad = TEXT // 16 * 16

    def spread(block):
        @pl.when(block == 0)
        def _():
            own[2].wait()
            zero = jnp.zeros((2, PATCH - text_pad, kv.shape[-1]), kv.dtype)
            kv[:, (PATCHES - 1) * PATCH + text_pad :, :] = zero
            ve[:, (PATCHES - 1) * PATCH + text_pad :, :] = zero

        def lanes_of(c):
            return pl.ds(pl.multiple_of(c * 2 * HD, 2 * HD), 2 * HD)

        @pl.when(block < PATCHES - 1)
        def _():
            begin = (block + (block >= patch_here).astype(jnp.int32)) * PATCH
            into = pl.ds(pl.multiple_of(block * PATCH, PATCH), PATCH)

            def body(c, _):
                pair = jnp.swapaxes(raw[pl.ds(begin, PATCH), :, lanes_of(c)], 0, 1)
                kv[:, into, lanes_of(c)] = pair
                ve[:, into, lanes_of(c)] = jnp.where(lane2 < HD, jnp.bfloat16(1), pair)
                return 0

            lax.fori_loop(0, heads_here, body, 0)

        @pl.when(block == PATCHES - 1)
        def _():
            first = (PATCHES - 1) * PATCH

            def body(c, _):
                pair = jnp.swapaxes(raw[PATCHES * PATCH :, :, lanes_of(c)], 0, 1)
                kv[:, first : first + TEXT, lanes_of(c)] = pair
                ve[:, first : first + TEXT, lanes_of(c)] = jnp.where(
                    lane2 < HD, jnp.bfloat16(1), pair
                )
                return 0

            lax.fori_loop(0, heads_here, body, 0)

    time_here = timestep[0]

    def modulation(k, r):
        return time_mod[time_here, k] + text_mod[k, pl.ds(r, 1), :]

    def normalised(r):
        values_f = hbuf[r].astype(jnp.float32)
        row_mean = jnp.mean(values_f, axis=-1, keepdims=True)
        centered = values_f - row_mean
        row_var = jnp.mean(centered * centered, axis=-1, keepdims=True)
        scaled = centered * lax.rsqrt(row_var + 1e-06)
        return (scaled * (1.0 + modulation(1, r)) + modulation(0, r)).astype(jnp.bfloat16)

    def onward(r, c, target):
        lanes = pl.ds(c * chunk, chunk)
        return pltpu.make_async_remote_copy(
            src_ref=mine.at[r, :, lanes],
            dst_ref=hbuf.at[r, own_rows, lanes],
            send_sem=x_send.at[r, c],
            recv_sem=x_recv.at[r, c],
            device_id={"section": target},
            device_id_type=MESH,
        )

    def forward(r, c, far, owner):
        into = pl.ds(pl.multiple_of(owner * rows, rows), rows)
        lanes = pl.ds(c * chunk, chunk)
        return pltpu.make_async_remote_copy(
            src_ref=hbuf.at[r, into, lanes],
            dst_ref=hbuf.at[r, into, lanes],
            send_sem=f_send.at[r, c, far - 1],
            recv_sem=f_recv.at[r, c, far - 1],
            device_id={"head": (head + far) % heads},
            device_id_type=MESH,
        )

    keep = [jnp.float32(1.0), (guided[0] != 0).astype(jnp.float32)]
    lane = lax.broadcasted_iota(jnp.int32, (PATCH, PATCH), 1)
    lane1 = lax.broadcasted_iota(jnp.int32, (PATCH, 2 * HD), 1)
    blank = jnp.zeros((PATCH, HD), jnp.bfloat16)

    def columns_of(j):
        return pl.ds(pl.multiple_of(j * span, 128), span) if groups > 1 else slice(None)

    def lanes_of(j, h):
        return pl.ds(pl.multiple_of((j * group + h) * 2 * HD, 2 * HD), 2 * HD)

    def score(r, j, h, projected, slot):
        query = projected[:, h * 3 * HD : h * 3 * HD + HD]
        pair = projected[:, h * 3 * HD + HD : (h + 1) * 3 * HD]
        query = jnp.concatenate([query * jnp.bfloat16(HD**-0.5), blank], axis=1)
        most = None
        for b in range(PATCHES + 1):
            part = pair if b == 0 else kv[r, (b - 1) * PATCH : b * PATCH, lanes_of(j, h)]
            block = nt_dot(query, part)
            if b == PATCHES:
                cut_at = TEXT // 128 * 128
                tail = jnp.where(lane[:, cut_at:] < TEXT, block[:, cut_at:], -jnp.inf)
                block = jnp.concatenate([block[:, :cut_at], tail], axis=1)
            scores[slot, :, b * PATCH : (b + 1) * PATCH] = block
            here = jnp.maximum(block[:, :128], block[:, 128:])
            most = here if most is None else jnp.maximum(most, here)
        tops[slot] = jnp.broadcast_to(jnp.max(most, axis=-1, keepdims=True), (PATCH, 128))

    def mix(r, j, h, projected, slot):
        keep_here = jnp.where(r == 0, keep[0], keep[1])
        pair = projected[:, h * 3 * HD + HD : (h + 1) * 3 * HD]
        fresh_out[r, :, lanes_of(j, h)] = (pair.astype(jnp.float32) * keep_here).astype(
            jnp.bfloat16
        )
        top = tops[slot]
        top = jnp.concatenate([top, top], axis=1)
        total = None
        for b in range(PATCHES + 1):
            if b == 0:
                value = jnp.where(lane1 < HD, jnp.bfloat16(1), pair)
            else:
                value = ve[r, (b - 1) * PATCH : b * PATCH, lanes_of(j, h)]
            weight = jnp.exp(scores[slot, :, b * PATCH : (b + 1) * PATCH] - top)
            term = jnp.dot(weight.astype(jnp.bfloat16), value, preferred_element_type=jnp.float32)
            total = term if total is None else total + term
        return (total[:, HD:] / total[:, :HD]).astype(jnp.bfloat16)

    def attend(r, project, beside):
        first = project(r, 0)
        pscr[...] = first
        score(r, 0, 0, first, 0)

        def group_body(j, _):
            beside(j)
            projected = pscr[...]
            outs = []
            if groups > 1:
                following = jnp.minimum(j + 1, groups - 1)
                later = project(r, following)
            for h in range(group):
                if h + 1 < group:
                    score(r, j, h + 1, projected, (h + 1) % 2)
                elif groups > 1:
                    score(r, following, 0, later, 0)
                outs.append(mix(r, j, h, projected, h % 2))
            if groups > 1:
                pscr[...] = later
                cols = pl.ds(pl.multiple_of(j * group * HD, 128), group * HD)
            else:
                cols = slice(None)
            mixed[r, :, cols] = jnp.concatenate(outs, axis=1)
            return 0

        lax.fori_loop(0, groups, group_body, 0)

    def share(r, c, far):
        peer = (head + far) % heads
        lanes = pl.ds(c * chunk, chunk)
        return pltpu.make_async_remote_copy(
            src_ref=terms.at[r, pl.ds(pl.multiple_of(peer * rows, rows), rows), lanes],
            dst_ref=inbox.at[far - 1, r, :, lanes],
            send_sem=e_send.at[r, c, far - 1],
            recv_sem=e_recv.at[r, c, far - 1],
            device_id={"head": peer},
            device_id_type=MESH,
        )

    def finish(r, c, sends):
        lanes = slice(c * chunk, (c + 1) * chunk)
        attn = terms[r, own_rows, lanes].astype(jnp.float32)
        for far in range(1, heads):
            share(r, c, far).wait_recv()
            attn = attn + inbox[far - 1, r, :, lanes].astype(jnp.float32)
        before = hbuf[r, own_rows, lanes].astype(jnp.float32)
        gate = modulation(2, r)[:, lanes]
        updated = (before + gate * attn).astype(jnp.bfloat16)
        hidden_out[r, :, lanes] = (updated.astype(jnp.float32) * keep[r]).astype(jnp.bfloat16)
        if sends:
            mine[r, :, lanes] = updated
            onward(r, c, 1).start()

    blocks = chunk // o_rows

    def put_out(some_rows, sends, lag):
        steps = [(r, c) for r in some_rows for c in range(chunks)]
        if len(some_rows) == 2:
            steps = [(None, c) for c in range(chunks)]
        waiting = []
        for r, c in steps:
            lanes = slice(c * chunk, (c + 1) * chunk)
            weight = wo[c * blocks : (c + 1) * blocks].reshape(chunk, wo.shape[2])
            if r is None:
                both = mixed[...].reshape(2 * PATCH, wo.shape[2])
                term = nt_dot(both, weight).astype(jnp.bfloat16)
                terms[:, :, lanes] = term.reshape(2, PATCH, chunk)
            else:
                terms[r, :, lanes] = nt_dot(mixed[r], weight).astype(jnp.bfloat16)
            for row in range(2) if r is None else [r]:
                for far in range(1, heads):
                    share(row, c, far).start()
                waiting.append((row, c))
            while len(waiting) > lag:
                finish(*waiting.pop(0), sends)
        for row, c in waiting:
            finish(row, c, sends)

    everything = [(r, c) for r in range(2) for c in range(chunks)]

    @pl.when(section == 0)
    def _():
        lend(1).start()
        for r in range(2):
            for far in range(1, heads):
                token_copy(r, far, head).start()
        time_copy.wait()
        cuts = (cut_0, cut_1)
        places = [
            (way[0][0], sum(count for _, count in way)) if way else None for way in q_spans
        ]
        for r in range(2):
            own_tokens[r].wait()
            for far in range(1, heads):
                token_copy(r, far, (head + heads - far) % heads).wait_recv()
            normed[...] = normalised(r)
            for way in range(2):
                if places[way] is not None:
                    begin, count = places[way]
                    for o in range(n):
                        cuts[way][o, r * PATCH : (r + 1) * PATCH, :] = normed[
                            :, o * q_rows + begin : o * q_rows + begin + count
                        ]

        tile = 768 if qkv_columns % 768 == 0 else qkv_columns

        def add_up(owner, way, start):
            if places[way] is None:
                return
            begin, count = places[way]

            def body(t, _):
                cols = (
                    pl.ds(pl.multiple_of(t * tile, 128), tile)
                    if tile < qkv_columns
                    else slice(None)
                )
                term = jnp.dot(
                    cuts[way][owner],
                    wq[owner, begin : begin + count, cols],
                    preferred_element_type=jnp.float32,
                )
                if start:
                    projected_all[:, cols] = term
                else:
                    projected_all[:, cols] += term
                return 0

            lax.fori_loop(0, qkv_columns // tile, body, 0)

        own[0].wait()
        for way in range(2):
            add_up(me, way, way == 0)

        def arrived(step):
            for way in range(2):
                owner = ring_index((place + (n - step if way == 0 else step)) % n, n)
                add_up(owner, way, False)

        lead = n // 8

        def q_step(step, _):
            relay(q_ring, step)

            @pl.when(step == lead)
            def _():
                begin_ring(part_ring)

            @pl.when(step > lead)
            def _():
                relay(part_ring, step - lead)

            spread(step - 1)
            arrived(step)
            return 0

        lax.fori_loop(1, n - 1, q_step, 0)
        own[1].wait()
        settle(q_ring)
        relay(part_ring, n - 1 - lead)
        arrived(n - 1)

        def project(r, j):
            begin = pl.ds(pl.multiple_of(r * PATCH, PATCH), PATCH)
            return projected_all[begin, columns_of(j)].astype(jnp.bfloat16)

        def beside(j):
            low = jnp.minimum(j * (lead - 1) // 2, lead - 1)
            high = jnp.minimum((j + 1) * (lead - 1) // 2, lead - 1)
            relays(part_ring, n - lead + low, n - lead + high)

        attend(0, project, beside)
        relays(part_ring, n - lead + jnp.minimum(groups * (lead - 1) // 2, lead - 1), n - 1)
        write_fresh(0).start()
        settle(part_ring)

        def back(step, _):
            for way, k in order_of(x_spans):
                give_back(step, way, k, 1).wait_recv()
            return 0

        lax.fori_loop(0, n - 1, back, 0)
        put_out([0], True, 1)
        write_hidden(0).start()
        attend(1, project, lambda j: None)
        write_fresh(1).start()
        put_out([1], True, 1)
        write_hidden(1).start()
        for r in range(2):
            for far in range(1, heads):
                token_copy(r, far, head).wait_send()
        for r, c in everything:
            onward(r, c, 1).wait_send()
        lend(1).wait_send()

    @pl.when(section == 1)
    def _():
        lend(0).wait_recv()
        begin_ring(x_ring)

        def hand_back(step):
            for way, k in order_of(x_spans):
                give_back(step, way, k, 0).start()

        def x_step(step):
            @pl.when(step < n - 1)
            def _():
                relay(x_ring, step)
                hand_back(step - 1)

            @pl.when(step == n - 1)
            def _():
                settle(x_ring)
                hand_back(n - 2)

        lead = n // 2
        q_first = [kind for kind in q_ring[1] if kind[1] == 0]
        q_rest = [kind for kind in q_ring[1] if kind[1] > 0]

        def q_step(step, _):
            x_step(2 * step - 1)
            relay((q_ring[0], q_first), step)
            x_step(2 * step)
            relay((q_ring[0], q_rest), step)

            @pl.when(step == lead)
            def _():
                begin_ring(whole_ring)

            @pl.when(step > lead)
            def _():
                relay(whole_ring, step - lead)

            spread(step - 1)
            return 0

        lax.fori_loop(1, n - 1, q_step, 0)
        own[1].wait()
        time_copy.wait()
        settle(q_ring)
        own[0].wait()
        early = n - lead
        relays(whole_ring, n - 1 - lead, early)

        def project(r, j):
            weight = wq[:, :, columns_of(j)].reshape(n * q_rows, span)
            return jnp.dot(normed[...], weight, preferred_element_type=jnp.float32).astype(
                jnp.bfloat16
            )

        def row_body(r, _):
            for c in range(chunks):
                onward(r, c, 0).wait_recv()
                for far in range(1, heads):
                    forward(r, c, far, head).start()
            for c in range(chunks):
                for far in range(1, heads):
                    forward(r, c, far, (head + heads - far) % heads).wait_recv()
            normed[...] = normalised(r)

            def beside(j):
                shift = groups * 2 // 3
                done = jnp.clip(r * groups + j - shift, 0, groups)
                later = jnp.clip(r * groups + j + 1 - shift, 0, groups)
                left_over = n - 1 - early
                relays(
                    whole_ring,
                    early + (done * left_over + groups - 1) // groups,
                    early + (later * left_over + groups - 1) // groups,
                )

            attend(r, project, beside)
            write_fresh(r).start()
            return 0

        lax.fori_loop(0, 2, row_body, 0)
        settle(whole_ring)
        put_out([0, 1], False, 4)
        for r in range(2):
            write_hidden(r).start()

        def handed(step, _):
            for way, k in order_of(x_spans):
                give_back(step, way, k, 0).wait_send()
            return 0

        lax.fori_loop(0, n - 1, handed, 0)
        for r, c in everything:
            for far in range(1, heads):
                forward(r, c, far, head).wait_send()

    for r, c in everything:
        for far in range(1, heads):
            share(r, c, far).wait_send()
    for r in range(2):
        write_fresh(r).wait()
        write_hidden(r).wait()


def shards(
    latent_tokens, w_qkv, w_out, time_mod, text_mod, stale_kv, guided, patch_index, timestep
):
    n = lax.axis_size("req")
    heads = lax.axis_size("head")
    rows, width = latent_tokens.shape[2:]
    columns = stale_kv.shape[-1]
    bf16, f32 = jnp.bfloat16, jnp.float32
    chunks = width // (384 if width % 384 == 0 else width)
    heads_here = columns // (2 * HD)
    group = heads_a_step(heads_here)
    dma = pltpu.SemaphoreType.DMA
    smem = pl.BlockSpec(memory_space=pltpu.SMEM)
    vmem = pl.BlockSpec(memory_space=pltpu.VMEM)
    hbm = pl.BlockSpec(memory_space=pl.ANY)
    keys = PATCHES * PATCH
    lent = lent_rows(w_out.shape[2])
    counts = [sum(count for _, count in way) for way in cut(0, w_qkv.shape[1])]
    hidden, fresh = pl.pallas_call(
        functools.partial(fused_kernel, n, heads),
        out_shape=(
            jax.ShapeDtypeStruct((2, rows, width), bf16),
            jax.ShapeDtypeStruct((2, PATCH, columns), bf16),
        ),
        in_specs=[smem, smem, smem, hbm, hbm, hbm, hbm, vmem, hbm],
        out_specs=[hbm, hbm],
        scratch_shapes=[
            pltpu.VMEM((2, rows, width), bf16),
            pltpu.VMEM((2, PATCH, columns), bf16),
            pltpu.VMEM((time_mod.shape[1], time_mod.shape[2], 1, width), f32),
            pltpu.VMEM((n, *w_qkv.shape[1:]), bf16),
            pltpu.VMEM((n, w_out.shape[2], w_out.shape[1]), bf16),
            pltpu.VMEM((n, lent, w_out.shape[1]), bf16),
            pltpu.VMEM((STALE, 2, columns), bf16),
            pltpu.VMEM((2, keys, columns), bf16),
            pltpu.VMEM((2, keys, columns), bf16),
            pltpu.VMEM((2, PATCH, width), bf16),
            pltpu.VMEM((PATCH, width), bf16),
            *[pltpu.VMEM((n, 2 * PATCH, max(16, count)), bf16) for count in counts],
            pltpu.VMEM((2 * PATCH, w_qkv.shape[2]), f32),
            pltpu.VMEM((2, PATCH, columns // 2), bf16),
            pltpu.VMEM((2, PATCH, keys + PATCH), f32),
            pltpu.VMEM((2, PATCH, 128), f32),
            pltpu.VMEM((PATCH, group * 3 * HD), bf16),
            pltpu.VMEM((2, PATCH, width), bf16),
            pltpu.VMEM((heads - 1, 2, rows, width), bf16),
            pltpu.VMEM((2, rows, width), bf16),
            dma((2, 2)),
            dma((n - 1, 2, 2)),
            dma((2, 2)),
            dma((n - 1, 2, 2)),
            dma((2, 2)),
            dma((n - 1, 2, 2)),
            dma((n - 1, 2, 2)),
            dma((n - 1, 2, 2)),
            dma((2,)),
            dma((10,)),
            dma((2, heads - 1)),
            dma((2, heads - 1)),
            dma((2, chunks, heads - 1)),
            dma((2, chunks, heads - 1)),
            dma((2, chunks)),
            dma((2, chunks)),
            dma((2, chunks, heads - 1)),
            dma((2, chunks, heads - 1)),
        ],
        compiler_params=pltpu.CompilerParams(
            collective_id=0, has_side_effects=True, vmem_limit_bytes=58 << 20
        ),
    )(
        timestep,
        patch_index,
        guided,
        latent_tokens[0],
        w_qkv[0],
        w_out[0].T,
        jnp.transpose(time_mod, (1, 2, 0, 3)),
        jnp.swapaxes(text_mod[0, 0], 0, 1),
        jnp.swapaxes(stale_kv[0, 0], 0, 1),
    )
    return (hidden[None, None], fresh[None, None])


def solution(mesh):
    in_specs = (
        P("req", None, "head", None),
        P("section", "req", "head"),
        P("section", "head", "req"),
        P("section", None, None, None),
        P("section", "req", None, None, None),
        P("section", "req", None, None, "head"),
        P("req"),
        P("req"),
        P("req"),
    )
    out_specs = (P("section", "req", None, "head", None), P("section", "req", None, None, "head"))
    return jax.shard_map(shards, mesh=mesh, in_specs=in_specs, out_specs=out_specs, check_vma=False)
```
